32 devices in a mesh: dp: 8 (over z, y), seq: 4 (over x, core).
Axes of the slice: x: 2, y: 2, z: 4, core: 2. Of those that a mesh axis runs over, the one named last changes fastest.
Arguments:
- inputs: bfloat16 [8, 1024, 1024], P('dp', 'seq'), may hold values from -6 to 6
- segments: int32 [8, 1024], P('dp'), may hold values from 0 to 5, never falling along the last dimension, each value on 1 to 768 neighbouring positions
- ln1_gain: bfloat16 [1024], P(('dp', 'seq')), may hold values from 0.25 to 1.75
- ln1_bias: bfloat16 [1024], P(('dp', 'seq')), may hold values from -1.75 to 1.75
- qkv_weight: bfloat16 [1024, 3072], P(('dp', 'seq'))
- query_bias: bfloat16 [1024], P(('dp', 'seq')), may hold values from -3 to 3
- value_bias: bfloat16 [1024], P(('dp', 'seq')), may hold values from -3 to 3
- out_weight: bfloat16 [1024, 1024], P(('dp', 'seq')), may hold values from -1.5 to 1.5
- out_bias: bfloat16 [1024], P(('dp', 'seq')), may hold values from -6 to 6
- ln2_gain: bfloat16 [1024], P(('dp', 'seq')), may hold values from 0.25 to 1.75
- ln2_bias: bfloat16 [1024], P(('dp', 'seq')), may hold values from -1.75 to 1.75
- up_weight: bfloat16 [1024, 4096], P(('dp', 'seq')), may hold values from -0.1875 to 0.1875
- up_bias: bfloat16 [4096], P(('dp', 'seq')), may hold values from -3 to 3
- down_weight: bfloat16 [4096, 1024], P(('dp', 'seq')), may hold values from -0.09375 to 0.09375
- down_bias: bfloat16 [1024], P(('dp', 'seq')), may hold values from -8 to 8
- cotangent: bfloat16 [8, 1024, 1024], P('dp', 'seq'), may hold values from -6 to 6
Outputs:
- outputs: bfloat16 [8, 1024, 1024], P('dp', 'seq')
- input_grad: float32 [8, 1024, 1024], P('dp', 'seq')
- ln1_gain_grad: float32 [1024], P(('dp', 'seq'))
- ln1_bias_grad: float32 [1024], P(('dp', 'seq'))
- qkv_weight_grad: float32 [1024, 3072], P(('dp', 'seq'))
- query_bias_grad: float32 [1024], P(('dp', 'seq'))
- value_bias_grad: float32 [1024], P(('dp', 'seq'))
- out_weight_grad: float32 [1024, 1024], P(('dp', 'seq'))
- out_bias_grad: float32 [1024], P(('dp', 'seq'))
- ln2_gain_grad: float32 [1024], P(('dp', 'seq'))
- ln2_bias_grad: float32 [1024], P(('dp', 'seq'))
- up_weight_grad: float32 [1024, 4096], P(('dp', 'seq'))
- up_bias_grad: float32 [4096], P(('dp', 'seq'))
- down_weight_grad: float32 [4096, 1024], P(('dp', 'seq'))
- down_bias_grad: float32 [1024], P(('dp', 'seq'))
The draws below stay inside these ranges and needn't reach their ends.
Inputs may be any that keep to these rules, and one draw needn't show every extreme that they name: `segments`: along each packed sequence the document numbers never fall; each document holds 1 to 768 tokens, and in every sequence one document holds exactly 768.
All inputs are finite; a program needn't handle non-finite values.
Results may differ from the reference program's by a relative error of at most 0.02.
The reference program's roundings to bfloat16 on the way count: a program that leaves them out, or rounds other values in their place, can miss the bound.
Values may be sent and summed in bfloat16 or wider, within the bound.
No kernel may reach another device: no remote copies, remote signals or barrier semaphores. Data moves between devices by JAX's collectives and lax.ppermute only.
A program may use at most 128 MiB of HBM per device.

```python
import math
import jax
import jax.numpy as jnp
import numpy as np
from jax import lax

D = 1024
HEADS = 16
HEAD_DIM = 64
FF = 4096
LENGTH = 1024
DOCS = 6
DOC_MOST = 768
NSEQ = 8


def draw_qkv_weight(key, part):
    normal_part = jax.random.normal(key, (D, 3 * D), jnp.float32) * (1.0 / math.sqrt(D))
    return normal_part.astype(jnp.bfloat16)


def block_scale(own_key, dims, cuts, low, largest):
    factor_of, own = 1.0, jax.random.fold_in(own_key, 6)
    for axis_at, blocks in cuts:
        heights = jnp.exp(jax.random.uniform(jax.random.fold_in(own, axis_at), (blocks,), jnp.float32, low / len(cuts), largest / len(cuts)))
        factor_of = factor_of * jnp.repeat(heights, dims[axis_at] // blocks).reshape([-1 if axis == axis_at else 1 for axis in range(len(dims))])
    return factor_of


def length_profile(amount, total, most, lean):
    weights = [(1 << 20) // math.isqrt(rank ** lean) + 1 for rank in range(2, amount + 1)]
    spare, counts = total - most - (amount - 1), [1] * (amount - 1)
    while spare > 0:
        candidates = [i for i in range(amount - 1) if counts[i] < most]
        mass, remaining = sum([weights[i] for i in candidates]), spare
        for i in candidates:
            extra = min(most - counts[i], max(1, remaining * weights[i] // mass), spare)
            counts[i] = counts[i] + extra
            spare = spare - extra
    return np.array([most] + counts)


def uneven_parts(rng, count, total, reach, lean):
    if count == 2:
        one = jax.random.randint(rng, (), max(1, total - reach), min(reach, total - 1) + 1)
        return jnp.stack([one, total - one])
    lengths = jnp.asarray(length_profile(count, total, reach, lean), jnp.int32)
    twos = (count - 1) // 2
    giver, taker = lengths[1:1 + 2 * twos:2], lengths[2:2 + 2 * twos:2]
    room = jnp.minimum(giver - 1, reach - taker)
    passed = jax.random.randint(jax.random.fold_in(rng, 1), (twos,), 0, 1 << 20) % (room + 1)
    lengths = lengths.at[1:1 + 2 * twos:2].set(giver - passed).at[2:2 + 2 * twos:2].set(taker + passed)
    return lengths[jax.random.permutation(jax.random.fold_in(rng, 2), count)]


def scatter_about(key, extent, scale, most, split=(), kind=jnp.bfloat16):
    values = jax.random.normal(key, extent, jnp.float32) * scale
    if len(split) > 0:
        values = block_scale(key, extent, split, -0.22, 0.18) * values
    return jnp.clip(values, min=-most, max=most).astype(kind)


def setup_inputs(seed: int = 0) -> dict:
    arg_keys = jax.random.split(jax.random.key(seed), 17)
    inputs = scatter_about(arg_keys[0], (NSEQ, LENGTH, D), 1.0, 6.0, ((0, 8), (1, 4)))
    segments = jax.vmap(lambda own: jnp.searchsorted(jnp.cumsum(uneven_parts(own, DOCS, LENGTH, DOC_MOST, 2)), jnp.arange(LENGTH), side="right"))(jax.random.split(arg_keys[1], NSEQ)).reshape((NSEQ, LENGTH)).astype(jnp.int32)
    ln1_gain = jnp.clip(1.0 + 0.15 * jax.random.normal(arg_keys[2], (D,), jnp.float32), 0.25, 1.75).astype(jnp.bfloat16)
    ln1_bias = scatter_about(arg_keys[3], (D,), 0.3, 1.75, ((0, 32),))
    qkv_weight = draw_qkv_weight(jax.random.fold_in(arg_keys[16], 71), 0)
    query_bias = scatter_about(arg_keys[5], (D,), 0.5, 3.0, ((0, 32),))
    value_bias = scatter_about(arg_keys[6], (D,), 0.5, 3.0, ((0, 32),))
    out_weight = scatter_about(arg_keys[7], (D, D), (D // 64) ** -0.5, 1.5, ((0, 32),))
    out_bias = scatter_about(arg_keys[8], (D,), 1.0, 6.0, ((0, 32),))
    ln2_gain = jnp.clip(1.0 + 0.15 * jax.random.normal(arg_keys[9], (D,), jnp.float32), 0.25, 1.75).astype(jnp.bfloat16)
    ln2_bias = scatter_about(arg_keys[10], (D,), 0.3, 1.75, ((0, 32),))
    up_weight = scatter_about(arg_keys[11], (D, FF), D ** -0.5, 0.1875, ((0, 32),))
    up_bias = scatter_about(arg_keys[12], (FF,), 0.5, 3.0, ((0, 32),))
    down_weight = scatter_about(arg_keys[13], (FF, D), FF ** -0.5, 0.09375, ((0, 32),))
    down_bias = scatter_about(arg_keys[14], (D,), 1.5, 8.0, ((0, 32),))
    cotangent = scatter_about(arg_keys[15], (NSEQ, LENGTH, D), 1.0, 6.0, ((0, 8), (1, 4)))
    return {"inputs": inputs, "segments": segments, "ln1_gain": ln1_gain, "ln1_bias": ln1_bias, "qkv_weight": qkv_weight, "query_bias": query_bias, "value_bias": value_bias, "out_weight": out_weight, "out_bias": out_bias, "ln2_gain": ln2_gain, "ln2_bias": ln2_bias, "up_weight": up_weight, "up_bias": up_bias, "down_weight": down_weight, "down_bias": down_bias, "cotangent": cotangent}


EPSILON = 1e-05
SCORE_SCALE = 0.125
GELU_SCALE = 0.7978845608028654
GELU_CUBIC = 0.044715

def layer_norm(values_in, gain_term, bias_term):
    center = lax.optimization_barrier(jnp.mean(values_in, axis=-1, keepdims=True))
    offset = values_in - center
    spread = lax.optimization_barrier(jnp.mean(offset * offset, axis=-1, keepdims=True))
    inverse = lax.rsqrt(spread + EPSILON)
    normed = offset * inverse
    return (normed * gain_term.astype(jnp.float32) + bias_term.astype(jnp.float32), normed, inverse)

def layer_norm_back(upstream, normed, inverse, gain_term):
    scaled = upstream * gain_term.astype(jnp.float32)
    mean_grad = lax.optimization_barrier(jnp.mean(scaled, axis=-1, keepdims=True))
    mean_proj = lax.optimization_barrier(jnp.mean(scaled * normed, axis=-1, keepdims=True))
    return inverse * (scaled - mean_grad - normed * mean_proj)

def gelu_pair(preact):
    tanh_arg = GELU_SCALE * (preact + GELU_CUBIC * preact * preact * preact)
    tanh_val = jnp.tanh(tanh_arg)
    activated = 0.5 * preact * (1.0 + tanh_val)
    derivative = 0.5 * (1.0 + tanh_val) + 0.5 * preact * (1.0 - tanh_val * tanh_val) * GELU_SCALE * (1.0 + 3.0 * GELU_CUBIC * preact * preact)
    return (activated, derivative)

def attend(query_heads, key_heads, value_heads, visible):

    def one_head(operands):
        query_head, key_head, value_head = operands
        scores = jnp.einsum('sqd,skd->sqk', query_head.astype(jnp.float32), key_head.astype(jnp.float32)) * SCORE_SCALE
        scores = jnp.where(visible, scores, -jnp.inf)
        row_max = lax.optimization_barrier(jnp.max(scores, axis=-1, keepdims=True))
        weights = jnp.exp(scores - row_max)
        row_total = lax.optimization_barrier(jnp.sum(weights, axis=-1, keepdims=True))
        probability = (weights / row_total).astype(jnp.bfloat16)
        head_out = jnp.einsum('sqk,skd->sqd', probability.astype(jnp.float32), value_head.astype(jnp.float32))
        return (head_out.astype(jnp.bfloat16), (row_max + jnp.log(row_total))[..., 0])
    return lax.map(one_head, (query_heads, key_heads, value_heads))

def attend_back(query_heads, key_heads, value_heads, out_heads, grad_heads, log_totals, visible):

    def one_head(operands):
        query_head, key_head, value_head, out_head, grad_head, log_total = operands
        grad_wide = grad_head.astype(jnp.float32)
        scores = jnp.einsum('sqd,skd->sqk', query_head.astype(jnp.float32), key_head.astype(jnp.float32)) * SCORE_SCALE
        scores = jnp.where(visible, scores, -jnp.inf)
        probability = jnp.exp(scores - log_total[..., None])
        prob_half = probability.astype(jnp.bfloat16).astype(jnp.float32)
        value_grad = jnp.einsum('sqk,sqd->skd', prob_half, grad_wide)
        prob_grad = jnp.einsum('sqd,skd->sqk', grad_wide, value_head.astype(jnp.float32))
        row_dot = lax.optimization_barrier(jnp.sum(grad_wide * out_head.astype(jnp.float32), axis=-1, keepdims=True))
        score_grad = (probability * (prob_grad - row_dot) * SCORE_SCALE).astype(jnp.bfloat16).astype(jnp.float32)
        query_grad = jnp.einsum('sqk,skd->sqd', score_grad, key_head.astype(jnp.float32))
        key_grad = jnp.einsum('sqk,sqd->skd', score_grad, query_head.astype(jnp.float32))
        return (query_grad, key_grad, value_grad)
    return lax.map(one_head, (query_heads, key_heads, value_heads, out_heads, grad_heads, log_totals))

def reference(inputs, segments, ln1_gain, ln1_bias, qkv_weight, query_bias, value_bias, out_weight, out_bias, ln2_gain, ln2_bias, up_weight, up_bias, down_weight, down_bias, cotangent):
    key_place = jnp.arange(LENGTH, dtype=jnp.int32)
    causal = key_place[None, :] <= key_place[:, None]

    def split_heads(tensor):
        return tensor.reshape(1, LENGTH, HEADS, HEAD_DIM).transpose(2, 0, 1, 3)

    def merge_heads(tensor):
        return tensor.transpose(1, 2, 0, 3).reshape(LENGTH, D)

    def one_sequence(totals, operands):
        tokens, seg_row, upstream = operands
        visible = ((seg_row[:, None] == seg_row[None, :]) & causal)[None]
        hidden_in = tokens.astype(jnp.float32)
        normed_one, unit_one, inverse_one = layer_norm(hidden_in, ln1_gain, ln1_bias)
        normed_one = normed_one.astype(jnp.bfloat16)
        projected = jnp.dot(normed_one, qkv_weight, preferred_element_type=jnp.float32)
        queries = (projected[:, :D] + query_bias.astype(jnp.float32)).astype(jnp.bfloat16)
        keys_all = projected[:, D:2 * D].astype(jnp.bfloat16)
        values_all = (projected[:, 2 * D:] + value_bias.astype(jnp.float32)).astype(jnp.bfloat16)
        query_heads = split_heads(queries)
        key_heads = split_heads(keys_all)
        value_heads = split_heads(values_all)
        head_out, log_totals = attend(query_heads, key_heads, value_heads, visible)
        attended = merge_heads(head_out)
        residual_one = hidden_in + jnp.dot(attended, out_weight, preferred_element_type=jnp.float32) + out_bias.astype(jnp.float32)
        normed_two, unit_two, inverse_two = layer_norm(residual_one, ln2_gain, ln2_bias)
        normed_two = normed_two.astype(jnp.bfloat16)
        preact = jnp.dot(normed_two, up_weight, preferred_element_type=jnp.float32) + up_bias.astype(jnp.float32)
        activated, derivative = gelu_pair(preact)
        activated = activated.astype(jnp.bfloat16)
        outputs = (residual_one + jnp.dot(activated, down_weight, preferred_element_type=jnp.float32) + down_bias.astype(jnp.float32)).astype(jnp.bfloat16)
        upstream_wide = upstream.astype(jnp.float32)
        grad_down_w = jnp.dot(activated.T, upstream, preferred_element_type=jnp.float32)
        grad_down_b = lax.optimization_barrier(jnp.sum(upstream_wide, axis=0))
        preact_grad = jnp.dot(upstream, down_weight.T, preferred_element_type=jnp.float32) * derivative
        preact_half = preact_grad.astype(jnp.bfloat16)
        grad_up_w = jnp.dot(normed_two.T, preact_half, preferred_element_type=jnp.float32)
        grad_up_b = lax.optimization_barrier(jnp.sum(preact_grad, axis=0))
        normed_two_grad = jnp.dot(preact_half, up_weight.T, preferred_element_type=jnp.float32)
        grad_gain_two = lax.optimization_barrier(jnp.sum(normed_two_grad * unit_two, axis=0))
        grad_bias_two = lax.optimization_barrier(jnp.sum(normed_two_grad, axis=0))
        residual_grad = upstream_wide + layer_norm_back(normed_two_grad, unit_two, inverse_two, ln2_gain)
        residual_half = residual_grad.astype(jnp.bfloat16)
        grad_out_w = jnp.dot(attended.T, residual_half, preferred_element_type=jnp.float32)
        grad_out_b = lax.optimization_barrier(jnp.sum(residual_grad, axis=0))
        attended_grad = jnp.dot(residual_half, out_weight.T, preferred_element_type=jnp.float32).astype(jnp.bfloat16)
        query_grad, key_grad, value_grad = attend_back(query_heads, key_heads, value_heads, head_out, split_heads(attended_grad), log_totals, visible)
        query_flat = merge_heads(query_grad)
        key_flat = merge_heads(key_grad)
        value_flat = merge_heads(value_grad)
        qkv_half = jnp.concatenate([query_flat, key_flat, value_flat], axis=1).astype(jnp.bfloat16)
        grad_qkv_w = jnp.dot(normed_one.T, qkv_half, preferred_element_type=jnp.float32)
        grad_query_b = lax.optimization_barrier(jnp.sum(query_flat, axis=0))
        grad_value_b = lax.optimization_barrier(jnp.sum(value_flat, axis=0))
        normed_one_grad = jnp.dot(qkv_half, qkv_weight.T, preferred_element_type=jnp.float32)
        grad_gain_one = lax.optimization_barrier(jnp.sum(normed_one_grad * unit_one, axis=0))
        grad_bias_one = lax.optimization_barrier(jnp.sum(normed_one_grad, axis=0))
        input_grad = residual_grad + layer_norm_back(normed_one_grad, unit_one, inverse_one, ln1_gain)
        grads = (grad_gain_one, grad_bias_one, grad_qkv_w, grad_query_b, grad_value_b, grad_out_w, grad_out_b, grad_gain_two, grad_bias_two, grad_up_w, grad_up_b, grad_down_w, grad_down_b)
        return (jax.tree.map(jnp.add, totals, grads), (outputs, input_grad))
    params = (ln1_gain, ln1_bias, qkv_weight, query_bias, value_bias, out_weight, out_bias, ln2_gain, ln2_bias, up_weight, up_bias, down_weight, down_bias)
    zeros = tuple((jnp.zeros(param.shape, jnp.float32) for param in params))
    totals, stacked = lax.scan(one_sequence, zeros, (inputs, segments, cotangent))
    return (stacked[0], stacked[1], totals[0], totals[1], totals[2], totals[3], totals[4], totals[5], totals[6], totals[7], totals[8], totals[9], totals[10], totals[11], totals[12])
```

```python
import functools

import jax
import jax.numpy as jnp
from jax import lax
from jax.experimental import pallas as pl
from jax.experimental.pallas import tpu as pltpu
from jax.sharding import PartitionSpec as P

HEAD_DIM = 64


EPSILON = 1e-05
SCORE_SCALE = 0.125
GELU_SCALE = 0.7978845608028654
GELU_CUBIC = 0.044715


def layer_norm(values_in, gain_term, bias_term):
    center = jnp.mean(values_in, axis=-1, keepdims=True)
    offset = values_in - center
    spread = jnp.mean(offset * offset, axis=-1, keepdims=True)
    inverse = lax.rsqrt(spread + EPSILON)
    normed = offset * inverse
    return (normed * gain_term.astype(jnp.float32) + bias_term.astype(jnp.float32), normed, inverse)


def layer_norm_back(upstream, normed, inverse, gain_term):
    scaled = upstream * gain_term.astype(jnp.float32)
    mean_grad = jnp.mean(scaled, axis=-1, keepdims=True)
    mean_proj = jnp.mean(scaled * normed, axis=-1, keepdims=True)
    return inverse * (scaled - mean_grad - normed * mean_proj)


def gelu_pair(preact):
    tanh_arg = GELU_SCALE * (preact + GELU_CUBIC * preact * preact * preact)
    tanh_val = jnp.tanh(tanh_arg)
    activated = 0.5 * preact * (1.0 + tanh_val)
    derivative = 0.5 * (1.0 + tanh_val) + 0.5 * preact * (
        1.0 - tanh_val * tanh_val
    ) * GELU_SCALE * (1.0 + 3.0 * GELU_CUBIC * preact * preact)
    return (activated, derivative)


def split_heads(tensor):
    return tensor.reshape(tensor.shape[0], tensor.shape[1], -1, HEAD_DIM).transpose(2, 0, 1, 3)


def merge_heads(tensor):
    return tensor.transpose(1, 2, 0, 3).reshape(tensor.shape[1], tensor.shape[2], -1)


def attend(query_heads, key_heads, value_heads, visible):

    def one_head(operands):
        query_head, key_head, value_head = operands
        scores = (
            jnp.einsum("sqd,skd->sqk", query_head, key_head, preferred_element_type=jnp.float32)
            * SCORE_SCALE
        )
        scores = jnp.where(visible, scores, -jnp.inf)
        row_max = jnp.max(scores, axis=-1, keepdims=True)
        weights = jnp.exp(scores - row_max)
        row_total = jnp.sum(weights, axis=-1, keepdims=True)
        probability = (weights / row_total).astype(jnp.bfloat16)
        head_out = jnp.einsum(
            "sqk,skd->sqd", probability, value_head, preferred_element_type=jnp.float32
        )
        return (head_out.astype(jnp.bfloat16), (row_max + jnp.log(row_total))[..., 0])

    return lax.map(one_head, (query_heads, key_heads, value_heads))


def attend_back(query_heads, key_heads, value_heads, out_heads, grad_heads, log_totals, visible):

    def one_head(operands):
        query_head, key_head, value_head, out_head, grad_head, log_total = operands
        scores = (
            jnp.einsum("sqd,skd->sqk", query_head, key_head, preferred_element_type=jnp.float32)
            * SCORE_SCALE
        )
        scores = jnp.where(visible, scores, -jnp.inf)
        probability = jnp.exp(scores - log_total[..., None])
        prob_half = probability.astype(jnp.bfloat16)
        value_grad = jnp.einsum(
            "sqk,sqd->skd", prob_half, grad_head, preferred_element_type=jnp.float32
        )
        prob_grad = jnp.einsum(
            "sqd,skd->sqk", grad_head, value_head, preferred_element_type=jnp.float32
        )
        row_dot = jnp.sum(
            grad_head.astype(jnp.float32) * out_head.astype(jnp.float32), axis=-1, keepdims=True
        )
        score_grad = (probability * (prob_grad - row_dot) * SCORE_SCALE).astype(jnp.bfloat16)
        query_grad = jnp.einsum(
            "sqk,skd->sqd", score_grad, key_head, preferred_element_type=jnp.float32
        )
        key_grad = jnp.einsum(
            "sqk,sqd->skd", score_grad, query_head, preferred_element_type=jnp.float32
        )
        return (query_grad, key_grad, value_grad)

    return lax.map(
        one_head, (query_heads, key_heads, value_heads, out_heads, grad_heads, log_totals)
    )


def swap(tensor, axis, mask):
    count = lax.axis_size(axis)
    return lax.ppermute(tensor, axis, [(i, i ^ mask) for i in range(count)])


def inner_of(count):
    inner = 1
    while (inner * 2) ** 2 <= count and count % (inner * 2) == 0:
        inner *= 2
    return inner


def unxor(pieces, me):
    count = len(pieces)
    stacked = list(pieces)
    bit = 1
    while bit < count:
        flipped = (me & bit) != 0
        stacked = [jnp.where(flipped, stacked[i ^ bit], stacked[i]) for i in range(count)]
        bit *= 2
    return jnp.stack(stacked)


def exchange_seq(piece_for, seq_me, seq_parts):
    return [piece_for(seq_me)] + [
        swap(piece_for(seq_me ^ k), "seq", k) for k in range(1, seq_parts)
    ]


def gather_dp(shard, dp_parts):
    inner = inner_of(dp_parts)
    found = {0: shard}
    for k in range(inner, dp_parts, inner):
        found[k] = swap(shard, "dp", k)
    for k in range(0, dp_parts, inner):
        for j in range(1, inner):
            found[k + j] = swap(found[k], "dp", j)
    return [found[k] for k in range(dp_parts)]


def scatter_dp(blocks, dp_me, dp_parts):
    inner = inner_of(dp_parts)

    def block(k):
        return lax.dynamic_index_in_dim(blocks, dp_me ^ k, 0, keepdims=False)

    total = None
    for k in reversed(range(0, dp_parts, inner)):
        part = block(k).astype(jnp.float32)
        for j in range(1, inner):
            part = part + swap(block(k + j), "dp", j).astype(jnp.float32)
        if k:
            part = swap(part.astype(blocks.dtype), "dp", k).astype(jnp.float32)
        total = part if total is None else total + part
    return total


def place_kernel(dp_parts, seq_parts, rows, where_ref, *refs):
    ins, outs = refs[:dp_parts], refs[dp_parts:]
    far, near = pl.program_id(0), pl.program_id(1)
    for k in range(dp_parts):

        @pl.when(far == k)
        def _():
            outs[0][...] = ins[k][near, :rows, :][None, None]
            if len(outs) > 1:
                outs[1][...] = ins[k][near, rows:, :][None, None]


def place(blocks, rows, dp_me, seq_me):
    dp_parts = len(blocks)
    seq_parts, all_rows, columns = blocks[0].shape
    heights = [rows] + ([all_rows - rows] if all_rows > rows else [])
    outs = pl.pallas_call(
        functools.partial(place_kernel, dp_parts, seq_parts, rows),
        grid_spec=pltpu.PrefetchScalarGridSpec(
            num_scalar_prefetch=1,
            grid=(dp_parts, seq_parts),
            in_specs=[
                pl.BlockSpec((seq_parts, all_rows, columns), lambda i, j, at: (0, 0, 0))
                for _ in blocks
            ],
            out_specs=[
                pl.BlockSpec((1, 1, height, columns), lambda i, j, at: (at[0] ^ i, at[1] ^ j, 0, 0))
                for height in heights
            ],
        ),
        out_shape=[
            jax.ShapeDtypeStruct((dp_parts, seq_parts, height, columns), blocks[0].dtype)
            for height in heights
        ],
        name="place",
    )(jnp.stack([dp_me, seq_me]).astype(jnp.int32), *blocks)
    return outs


def rows_in(tensor, seq_me):
    seq_parts = lax.axis_size("seq")
    found = {0: tensor}
    for k in range(2, seq_parts, 2):
        found[k] = swap(tensor, "seq", k)
    if seq_parts > 1:
        for k in range(0, seq_parts, 2):
            found[k + 1] = swap(found[k], "seq", 1)
    rows, columns = tensor.shape
    blocks = [found[k][None] for k in range(seq_parts)]
    (full,) = place(blocks, rows, seq_me, jnp.int32(0))
    return full.reshape(seq_parts * rows, columns)


def rows_out(term, seq_me):
    seq_parts = lax.axis_size("seq")
    blocks = term.reshape(seq_parts, -1, term.shape[1])

    def block(k):
        return lax.dynamic_index_in_dim(blocks, seq_me ^ k, 0, keepdims=False)

    total = None
    for k in reversed(range(0, seq_parts, 2)):
        part = block(k).astype(jnp.float32)
        part = part + swap(block(k + 1), "seq", 1).astype(jnp.float32)
        if k:
            part = swap(part.astype(term.dtype), "seq", k).astype(jnp.float32)
        total = part if total is None else total + part
    return total


def per_device(
    inputs,
    segments,
    ln1_gain,
    ln1_bias,
    qkv_weight,
    query_bias,
    value_bias,
    out_weight,
    out_bias,
    ln2_gain,
    ln2_bias,
    up_weight,
    up_bias,
    down_weight,
    down_bias,
    cotangent,
):
    half = jnp.bfloat16
    wide = jnp.float32
    seq_count, group_len, model_width = inputs.shape
    assert seq_count == 1
    full_len = segments.shape[1]
    dp_parts, seq_parts = lax.axis_size("dp"), lax.axis_size("seq")
    dp_me, seq_me = lax.axis_index("dp"), lax.axis_index("seq")
    head_width = model_width // seq_parts
    block = qkv_weight.shape[0]
    down_block = down_weight.shape[0]
    unit_width = dp_parts * down_block
    span = dp_parts // seq_parts

    vectors = jnp.concatenate(
        [
            ln1_gain,
            ln1_bias,
            query_bias,
            value_bias,
            out_bias,
            ln2_gain,
            ln2_bias,
            down_bias,
            up_bias,
        ]
    )
    vector_row = jnp.pad(vectors, (0, 3 * head_width - vectors.shape[0]))[None]
    qkv_view = qkv_weight.reshape(block, 3, seq_parts, head_width)

    def qkv_piece(t):
        columns = lax.dynamic_index_in_dim(qkv_view, t, 2, keepdims=False)
        return jnp.concatenate([columns.reshape(block, 3 * head_width), vector_row])

    qkv_mine = jnp.stack(exchange_seq(qkv_piece, seq_me, seq_parts))
    up_view = up_weight.reshape(block, dp_parts, seq_parts, down_block)

    def up_piece(t):
        return lax.dynamic_index_in_dim(up_view, t, 2, keepdims=False).reshape(block, unit_width)

    tokens = inputs.reshape(group_len, model_width)
    tokens_full = rows_in(tokens, seq_me)
    qkv_placed, vectors_placed = place(gather_dp(qkv_mine, dp_parts), block, dp_me, seq_me)
    qkv_cols = qkv_placed.reshape(model_width, 3, head_width)

    out_blocks = place(
        [b[None] for b in gather_dp(out_weight, dp_parts)], block, dp_me, jnp.int32(0)
    )[0].reshape(seq_parts, span * block, model_width)

    def out_piece(t):
        return lax.dynamic_index_in_dim(out_blocks, t, 0, keepdims=False)

    out_part = (
        unxor(exchange_seq(out_piece, seq_me, seq_parts), seq_me)
        .reshape(seq_parts, span, block, model_width)
        .transpose(1, 0, 2, 3)
        .reshape(head_width, model_width)
    )
    up_mine = jnp.stack(exchange_seq(up_piece, seq_me, seq_parts))
    up_cols = place(gather_dp(up_mine, dp_parts), block, dp_me, seq_me)[0].reshape(
        model_width, unit_width
    )
    down_part = place(
        [b[None] for b in gather_dp(down_weight, dp_parts)], down_block, dp_me, jnp.int32(0)
    )[0].reshape(unit_width, model_width)

    table = vectors_placed.reshape(dp_parts, seq_parts, 3 * head_width)
    (gain_one, bias_one, bias_query, bias_value, bias_out, gain_two, bias_two, bias_down) = (
        table[:, :, i * block : (i + 1) * block].reshape(model_width).astype(wide) for i in range(8)
    )
    bias_up = (
        lax.dynamic_index_in_dim(table, seq_me, 1, keepdims=False)[
            :, 8 * block : 8 * block + down_block
        ]
        .reshape(unit_width)
        .astype(wide)
    )
    query_part = lax.dynamic_slice_in_dim(bias_query, seq_me * head_width, head_width, 0)
    value_part = lax.dynamic_slice_in_dim(bias_value, seq_me * head_width, head_width, 0)

    upstream_full = rows_in(cotangent.reshape(group_len, model_width), seq_me)

    key_place = jnp.arange(full_len, dtype=jnp.int32)
    visible = (segments[:, :, None] == segments[:, None, :]) & (
        key_place[None, None, :] <= key_place[None, :, None]
    )
    normed_full = layer_norm(tokens_full.astype(wide), gain_one, bias_one)[0].astype(half)
    projected = jnp.einsum("rd,dch->rch", normed_full, qkv_cols, preferred_element_type=wide)
    queries = (projected[:, 0] + query_part).astype(half)[None]
    keys_mine = projected[:, 1].astype(half)[None]
    values_mine = (projected[:, 2] + value_part).astype(half)[None]
    query_heads = split_heads(queries)
    key_heads = split_heads(keys_mine)
    value_heads = split_heads(values_mine)
    head_out, log_totals = attend(query_heads, key_heads, value_heads, visible)
    attended = merge_heads(head_out).reshape(full_len, head_width)
    out_term = jnp.dot(attended, out_part, preferred_element_type=wide).astype(half)
    hidden_in = tokens.astype(wide)
    residual_one = hidden_in + rows_out(out_term, seq_me) + bias_out
    normed_two, unit_two, inverse_two = layer_norm(residual_one, gain_two, bias_two)
    normed_two_full = rows_in(normed_two.astype(half), seq_me)
    preact = jnp.dot(normed_two_full, up_cols, preferred_element_type=wide) + bias_up
    activated, derivative = gelu_pair(preact)
    activated = activated.astype(half)
    preact_grad = jnp.dot(upstream_full, down_part.T, preferred_element_type=wide) * derivative
    preact_half = preact_grad.astype(half)
    two_term = jnp.dot(preact_half, up_cols.T, preferred_element_type=wide).astype(half)
    normed_two_grad = rows_out(two_term, seq_me)
    grad_down = jnp.dot(activated.T, upstream_full, preferred_element_type=wide).astype(half)
    down_share = scatter_dp(grad_down.reshape(dp_parts, down_block, model_width), dp_me, dp_parts)
    grad_up = jnp.dot(normed_two_full.T, preact_half, preferred_element_type=wide).astype(half)
    up_rows = scatter_dp(
        grad_up.reshape(dp_parts, seq_parts * block, unit_width), dp_me, dp_parts
    ).astype(half)
    up_rows = up_rows.reshape(seq_parts, block, unit_width)
    up_share = (
        unxor(
            exchange_seq(
                lambda t: lax.dynamic_index_in_dim(up_rows, t, 0, keepdims=False), seq_me, seq_parts
            ),
            seq_me,
        )
        .reshape(seq_parts, block, dp_parts, down_block)
        .transpose(1, 2, 0, 3)
        .reshape(block, seq_parts * unit_width)
        .astype(wide)
    )
    down_term = jnp.dot(activated, down_part, preferred_element_type=wide).astype(half)
    outputs = (residual_one + rows_out(down_term, seq_me) + bias_down).astype(half)

    upstream_wide = cotangent.astype(wide).reshape(group_len, model_width)
    residual_grad = upstream_wide + layer_norm_back(
        normed_two_grad, unit_two, inverse_two, gain_two
    )
    residual_full = rows_in(residual_grad.astype(half), seq_me)
    attended_grad = jnp.dot(residual_full, out_part.T, preferred_element_type=wide).astype(half)
    grad_heads = split_heads(attended_grad[None])
    query_grad, key_grad, value_grad = attend_back(
        query_heads, key_heads, value_heads, head_out, grad_heads, log_totals, visible
    )
    query_flat = merge_heads(query_grad).reshape(full_len, head_width)
    key_flat = merge_heads(key_grad).reshape(full_len, head_width)
    value_flat = merge_heads(value_grad).reshape(full_len, head_width)
    qkv_half = jnp.concatenate([query_flat, key_flat, value_flat], axis=1).astype(half)
    grad_qkv = jnp.dot(normed_full.T, qkv_half, preferred_element_type=wide).astype(half)
    qkv_rows = (
        scatter_dp(grad_qkv.reshape(dp_parts, seq_parts * block, 3 * head_width), dp_me, dp_parts)
        .astype(half)
        .reshape(seq_parts, block, 3 * head_width)
    )
    qkv_share = (
        unxor(
            exchange_seq(
                lambda t: lax.dynamic_index_in_dim(qkv_rows, t, 0, keepdims=False),
                seq_me,
                seq_parts,
            ),
            seq_me,
        )
        .reshape(seq_parts, block, 3, head_width)
        .transpose(1, 2, 0, 3)
        .reshape(block, 3 * model_width)
        .astype(wide)
    )
    one_term = jnp.dot(
        qkv_half, qkv_cols.reshape(model_width, 3 * head_width).T, preferred_element_type=wide
    ).astype(half)
    normed_one_grad = rows_out(one_term, seq_me)
    _, unit_one, inverse_one = layer_norm(hidden_in, gain_one, bias_one)
    input_grad = residual_grad + layer_norm_back(normed_one_grad, unit_one, inverse_one, gain_one)

    grad_out = jnp.dot(attended.T, residual_full, preferred_element_type=wide).astype(half)
    grad_out = grad_out.reshape(span, seq_parts, block, model_width)
    out_found = unxor(
        exchange_seq(
            lambda t: lax.dynamic_index_in_dim(grad_out, t, 1, keepdims=False), seq_me, seq_parts
        ),
        seq_me,
    ).reshape(dp_parts, block, model_width)
    out_share = scatter_dp(out_found, dp_me, dp_parts)

    def place_part(part):
        return lax.dynamic_update_slice_in_dim(
            jnp.zeros((model_width,), wide), part, seq_me * head_width, 0
        )

    small = jnp.stack(
        [
            jnp.sum(normed_one_grad * unit_one, axis=0),
            jnp.sum(normed_one_grad, axis=0),
            place_part(jnp.sum(query_flat, axis=0)),
            place_part(jnp.sum(value_flat, axis=0)),
            jnp.sum(residual_grad, axis=0),
            jnp.sum(normed_two_grad * unit_two, axis=0),
            jnp.sum(normed_two_grad, axis=0),
            jnp.sum(upstream_wide, axis=0),
        ]
    )
    small = small.reshape(8, dp_parts, seq_parts, block).transpose(2, 1, 0, 3)
    small = small.reshape(seq_parts, dp_parts, 8 * block)
    small_mine = sum(
        exchange_seq(
            lambda t: lax.dynamic_index_in_dim(small, t, 0, keepdims=False), seq_me, seq_parts
        )
    )
    small_mine = jnp.concatenate(
        [small_mine, jnp.sum(preact_grad, axis=0).reshape(dp_parts, down_block)], axis=1
    )
    small_total = lax.dynamic_index_in_dim(small_mine, dp_me, 0, keepdims=False) + sum(
        swap(lax.dynamic_index_in_dim(small_mine, dp_me ^ k, 0, keepdims=False), "dp", k)
        for k in range(1, dp_parts)
    )
    shares = [small_total[i * block : (i + 1) * block] for i in range(8)]
    share_up_b = small_total[8 * block :]

    return (
        outputs[None],
        input_grad[None],
        shares[0],
        shares[1],
        qkv_share,
        shares[2],
        shares[3],
        out_share,
        shares[4],
        shares[5],
        shares[6],
        up_share,
        share_up_b,
        down_share,
        shares[7],
    )


def solution(mesh):
    spread = ("dp", "seq")
    vector, matrix, rows = P(spread), P(spread, None), P("dp", "seq", None)
    return jax.shard_map(
        per_device,
        mesh=mesh,
        in_specs=(
            rows,
            P("dp", None),
            vector,
            vector,
            matrix,
            vector,
            vector,
            matrix,
            vector,
            vector,
            vector,
            matrix,
            vector,
            matrix,
            vector,
            rows,
        ),
        out_specs=(
            rows,
            rows,
            vector,
            vector,
            matrix,
            vector,
            vector,
            matrix,
            vector,
            vector,
            vector,
            matrix,
            vector,
            matrix,
            vector,
        ),
        check_vma=False,
    )
```

```python
import functools

import jax
import jax.numpy as jnp
from jax import lax
from jax.experimental import pallas as pl
from jax.experimental.pallas import tpu as pltpu
from jax.sharding import PartitionSpec as P

HEAD_DIM = 64


EPSILON = 1e-05
SCORE_SCALE = 0.125
GELU_SCALE = 0.7978845608028654
GELU_CUBIC = 0.044715


def layer_norm(values_in, gain_term, bias_term):
    center = jnp.mean(values_in, axis=-1, keepdims=True)
    offset = values_in - center
    spread = jnp.mean(offset * offset, axis=-1, keepdims=True)
    inverse = lax.rsqrt(spread + EPSILON)
    normed = offset * inverse
    return (normed * gain_term.astype(jnp.float32) + bias_term.astype(jnp.float32), normed, inverse)


def layer_norm_back(upstream, normed, inverse, gain_term):
    scaled = upstream * gain_term.astype(jnp.float32)
    mean_grad = jnp.mean(scaled, axis=-1, keepdims=True)
    mean_proj = jnp.mean(scaled * normed, axis=-1, keepdims=True)
    return inverse * (scaled - mean_grad - normed * mean_proj)


def gelu_pair(preact):
    tanh_arg = GELU_SCALE * (preact + GELU_CUBIC * preact * preact * preact)
    tanh_val = jnp.tanh(tanh_arg)
    activated = 0.5 * preact * (1.0 + tanh_val)
    derivative = 0.5 * (1.0 + tanh_val) + 0.5 * preact * (
        1.0 - tanh_val * tanh_val
    ) * GELU_SCALE * (1.0 + 3.0 * GELU_CUBIC * preact * preact)
    return (activated, derivative)


def swap(tensor, axis, mask):
    count = lax.axis_size(axis)
    return lax.ppermute(tensor, axis, [(i, i ^ mask) for i in range(count)])


def inner_of(count):
    inner = 1
    while (inner * 2) ** 2 <= count and count % (inner * 2) == 0:
        inner *= 2
    return inner


def mask_order(count):
    inner = inner_of(count)
    return [k + j for j in range(inner) for k in range(0, count, inner)]


def place_by(pieces, at):
    count = len(pieces)
    stacked = list(pieces)
    bit = 1
    while bit < count:
        flipped = (at & bit) != 0
        stacked = [jnp.where(flipped, stacked[i ^ bit], stacked[i]) for i in range(count)]
        bit *= 2
    return jnp.stack(stacked)


def exchange_seq(piece_for, seq_me, seq_parts):
    return [piece_for(seq_me)] + [
        swap(piece_for(seq_me ^ k), "seq", k) for k in range(1, seq_parts)
    ]


def after(value, *earlier):
    return lax.optimization_barrier((value,) + earlier)[0]


def gather_outer(shard, dp_parts):
    inner = inner_of(dp_parts)
    return [shard] + [swap(shard, "dp", k) for k in range(inner, dp_parts, inner)]


def gather_inner(outer, dp_parts):
    inner = inner_of(dp_parts)
    cut = max(1, len(outer) // 2)
    groups = [b[None] for b in outer]
    sends = [jnp.stack(outer[:cut]), jnp.stack(outer[cut:])] if cut < len(outer) else [outer[0][None]]
    for j in range(1, inner):
        groups += [swap(s, "dp", j) for s in sends]
    return groups


def scatter_inner(blocks, dp_parts, *earlier):
    part = blocks[0].astype(jnp.float32)
    for j in range(1, inner_of(dp_parts)):
        came = swap(blocks[j], "dp", j)
        if earlier:
            came = after(came, *earlier)
        part = part + came.astype(jnp.float32)
    return part


def scatter_outer(part, dp_parts, dtype):
    inner = inner_of(dp_parts)
    sent = part.astype(dtype)
    return [part[0]] + [swap(sent[k], "dp", k * inner) for k in range(1, dp_parts // inner)]


def total_of(terms):
    total = terms[0]
    for term in terms[1:]:
        total = total + term.astype(jnp.float32)
    return total


def rows_far(tensor, seq_parts):
    return [swap(tensor, "seq", k) for k in range(2, seq_parts, 2)]


def rows_near(tensor, far, seq_parts):
    found = {0: tensor, 1: swap(tensor, "seq", 1)}
    for k in range(2, seq_parts, 2):
        found[k] = far[k // 2 - 1]
        found[k + 1] = swap(found[k], "seq", 1)
    return (
        jnp.concatenate([found[0], found[1]]),
        jnp.concatenate([found[k] for k in range(2, seq_parts)]),
    )


def rows_out(near, far, seq_parts):
    far = far.reshape(seq_parts - 2, -1, far.shape[1])
    near = near.reshape(2, -1, near.shape[1])
    total, sent = None, []
    for k in reversed(range(0, seq_parts, 2)):
        blocks, at = (far, k - 2) if k else (near, 0)
        part = blocks[at].astype(jnp.float32) + swap(blocks[at + 1], "seq", 1).astype(jnp.float32)
        if k:
            sent.append(part.astype(far.dtype))
            part = swap(sent[-1], "seq", k).astype(jnp.float32)
        total = part if total is None else total + part
    return total, sent


def place_dp(rows, dp_me, order):
    found = place_by([rows[i] for i in range(len(order))], dp_me)
    return jnp.stack([found[k] for k in order])


def qkv_place_kernel(sizes, seq_parts, rows, at_ref, *refs):
    ins, (main_ref, extra_ref) = refs[: len(sizes)], refs[len(sizes) :]
    dp_me, seq_me = at_ref[0], at_ref[1]
    order = mask_order(sum(sizes))
    spot = 0
    for ref, size in zip(ins, sizes):
        for g in range(size):
            far = dp_me ^ order[spot]
            for near in range(seq_parts):
                main_ref[far, seq_me ^ near] = ref[g, near, :rows, :]
                extra_ref[far, seq_me ^ near] = ref[g, near, rows:, :]
            spot += 1


def qkv_place(groups, rows, dp_parts, at):
    _, seq_parts, all_rows, columns = groups[0].shape
    sizes = [g.shape[0] for g in groups]
    wide = 256 if columns % 256 == 0 else columns
    return pl.pallas_call(
        functools.partial(qkv_place_kernel, sizes, seq_parts, rows),
        grid_spec=pltpu.PrefetchScalarGridSpec(
            num_scalar_prefetch=1,
            grid=(columns // wide,),
            in_specs=[
                pl.BlockSpec((size, seq_parts, all_rows, wide), lambda c, at: (0, 0, 0, c))
                for size in sizes
            ],
            out_specs=[
                pl.BlockSpec((dp_parts, seq_parts, height, wide), lambda c, at: (0, 0, 0, c))
                for height in (rows, all_rows - rows)
            ],
        ),
        out_shape=[
            jax.ShapeDtypeStruct((dp_parts, seq_parts, height, columns), groups[0].dtype)
            for height in (rows, all_rows - rows)
        ],
        name="qkv_place",
    )(at, *groups)


def out_place_kernel(sizes, at_ref, *refs):
    ins, out_ref = refs[: len(sizes)], refs[len(sizes)]
    order = mask_order(sum(sizes))
    spot = 0
    for ref, size in zip(ins, sizes):
        for g in range(size):
            out_ref[at_ref[0] ^ order[spot]] = ref[g]
            spot += 1


def out_place(groups, dp_parts, at):
    _, rows, columns = groups[0].shape
    full = pl.BlockSpec(memory_space=pltpu.VMEM)
    return pl.pallas_call(
        functools.partial(out_place_kernel, [g.shape[0] for g in groups]),
        in_specs=[pl.BlockSpec(memory_space=pltpu.SMEM)] + [full] * len(groups),
        out_specs=full,
        out_shape=jax.ShapeDtypeStruct((dp_parts, rows, columns), groups[0].dtype),
        name="out_place",
    )(at, *groups)


def up_place_kernel(sizes, seq_parts, units, at_ref, *refs):
    ins, up_ref = refs[: len(sizes)], refs[len(sizes)]
    dp_me, seq_me = at_ref[0], at_ref[1]
    order = mask_order(sum(sizes))
    spot = 0
    for ref, size in zip(ins, sizes):
        for g in range(size):
            far = dp_me ^ order[spot]
            for near in range(seq_parts):
                for m, mask in enumerate(order):
                    lanes = pl.ds(pl.multiple_of((dp_me ^ mask) * units, units), units)
                    up_ref[far, seq_me ^ near, :, m * units : (m + 1) * units] = ref[
                        g, near, :, lanes
                    ]
            spot += 1


def up_place(groups, dp_parts, units, at):
    _, seq_parts, rows, columns = groups[0].shape
    sizes = [g.shape[0] for g in groups]
    half = groups[0].dtype
    if units % 128 != 0:
        order = jnp.array(mask_order(dp_parts), jnp.int32)
        both = jnp.concatenate(groups)[jnp.argsort(order ^ at[0])]
        up = both[:, jnp.arange(seq_parts) ^ at[1]]
        up = up.reshape(dp_parts, seq_parts, rows, dp_parts, units)[:, :, :, order ^ at[0]]
        return up.reshape(dp_parts, seq_parts, rows, columns)
    return pl.pallas_call(
        functools.partial(up_place_kernel, sizes, seq_parts, units),
        grid_spec=pltpu.PrefetchScalarGridSpec(
            num_scalar_prefetch=1,
            grid=(1,),
            in_specs=[
                pl.BlockSpec((size, seq_parts, rows, columns), lambda c, at: (0, 0, 0, 0))
                for size in sizes
            ],
            out_specs=pl.BlockSpec(
                (dp_parts, seq_parts, rows, columns), lambda c, at: (0, 0, 0, 0)
            ),
        ),
        out_shape=jax.ShapeDtypeStruct((dp_parts, seq_parts, rows, columns), half),
        name="up_place",
    )(at, *groups)


def pair_width(width):
    return min(128, width)


def qkv_pieces_kernel(seq_parts, rows, depth, width, count, at_ref, w_ref, *refs):
    vectors, outs = refs[:count], refs[count:]
    lanes = pair_width(width)
    for k, out_ref in enumerate(outs):
        t = at_ref[1] ^ k
        for p in range(width // lanes):
            for c in range(3):
                source = pl.multiple_of(c * depth + t * width + p * lanes, lanes)
                to = (p * 3 + c) * lanes
                out_ref[:rows, to : to + lanes] = w_ref[:, pl.ds(source, lanes)]
        out_ref[rows:, :] = jnp.zeros((1, 3 * width), out_ref.dtype)
        spot = 0
        for ref in vectors:
            out_ref[rows:, spot : spot + ref.shape[1]] = ref[...]
            spot += ref.shape[1]


def qkv_pieces(weight, vectors, seq_parts, at):
    rows, columns = weight.shape
    depth = columns // 3
    width = depth // seq_parts
    full = pl.BlockSpec(memory_space=pltpu.VMEM)
    return pl.pallas_call(
        functools.partial(qkv_pieces_kernel, seq_parts, rows, depth, width, len(vectors)),
        in_specs=[pl.BlockSpec(memory_space=pltpu.SMEM), full] + [full] * len(vectors),
        out_specs=[full] * seq_parts,
        out_shape=[jax.ShapeDtypeStruct((rows + 1, 3 * width), weight.dtype)] * seq_parts,
        name="qkv_pieces",
    )(at, weight, *[v[None] for v in vectors])


def up_pieces_kernel(seq_parts, dp_parts, units, at_ref, w_ref, *outs):
    for k, out_ref in enumerate(outs):
        t = at_ref[1] ^ k
        for d in range(dp_parts):
            source = pl.multiple_of((d * seq_parts + t) * units, units)
            out_ref[:, d * units : (d + 1) * units] = w_ref[:, pl.ds(source, units)]


def up_pieces(weight, dp_parts, seq_parts, at):
    rows, columns = weight.shape
    units = columns // (dp_parts * seq_parts)
    width = dp_parts * units
    if units % 128 != 0:
        view = weight.reshape(rows, dp_parts, seq_parts, units)
        return [
            lax.dynamic_index_in_dim(view, at[1] ^ k, 2, keepdims=False).reshape(rows, width)
            for k in range(seq_parts)
        ]
    full = pl.BlockSpec(memory_space=pltpu.VMEM)
    return pl.pallas_call(
        functools.partial(up_pieces_kernel, seq_parts, dp_parts, units),
        in_specs=[pl.BlockSpec(memory_space=pltpu.SMEM), full],
        out_specs=[full] * seq_parts,
        out_shape=[jax.ShapeDtypeStruct((rows, width), weight.dtype)] * seq_parts,
        name="up_pieces",
    )(at, weight)


def up_finish_kernel(dp_parts, seq_parts, units, at_ref, *refs):
    out_ref = refs[-1]
    for k, ref in enumerate(refs[:-1]):
        for d in range(dp_parts):
            to = pl.multiple_of((d * seq_parts + (at_ref[1] ^ k)) * units, units)
            out_ref[:, pl.ds(to, units)] = ref[:, d * units : (d + 1) * units].astype(jnp.float32)


def up_finish(pieces, dp_parts, seq_parts, at):
    rows, width = pieces[0].shape
    units = width // dp_parts
    if units % 128 != 0:
        found = place_by(pieces, at[1]).reshape(seq_parts, rows, dp_parts, units)
        return found.transpose(1, 2, 0, 3).reshape(rows, seq_parts * width).astype(jnp.float32)
    full = pl.BlockSpec(memory_space=pltpu.VMEM)
    return pl.pallas_call(
        functools.partial(up_finish_kernel, dp_parts, seq_parts, units),
        in_specs=[pl.BlockSpec(memory_space=pltpu.SMEM)] + [full] * seq_parts,
        out_specs=full,
        out_shape=jax.ShapeDtypeStruct((rows, seq_parts * width), jnp.float32),
        name="up_finish",
    )(at, *pieces)


def up_pack_kernel(dp_parts, units, at_ref, *refs):
    ins, outs = refs[: len(refs) // 2], refs[len(refs) // 2 :]
    for in_ref, out_ref in zip(ins, outs):
        for m, mask in enumerate(mask_order(dp_parts)):
            lanes = pl.ds(pl.multiple_of((at_ref[0] ^ mask) * units, units), units)
            out_ref[0, :, lanes] = in_ref[0, :, m * units : (m + 1) * units]


def up_pack(grad, units, at):
    dp_parts, rows, columns = grad.shape
    inner = inner_of(dp_parts)
    outer = dp_parts // inner
    if units % 128 != 0:
        order = jnp.array(mask_order(dp_parts), jnp.int32)
        grad = grad[order ^ at[0]].reshape(dp_parts, rows, dp_parts, units)
        grad = grad[:, :, jnp.argsort(order ^ at[0])].reshape(dp_parts, rows, columns)
        return [grad[j * outer : (j + 1) * outer] for j in range(inner)]
    return pl.pallas_call(
        functools.partial(up_pack_kernel, dp_parts, units),
        grid_spec=pltpu.PrefetchScalarGridSpec(
            num_scalar_prefetch=1,
            grid=(outer,),
            in_specs=[
                pl.BlockSpec(
                    (1, rows, columns), functools.partial(lambda j, m, at: (at[0] ^ (m * inner + j), 0, 0), j)
                )
                for j in range(inner)
            ],
            out_specs=[pl.BlockSpec((1, rows, columns), lambda m, at: (m, 0, 0))] * inner,
        ),
        out_shape=[jax.ShapeDtypeStruct((outer, rows, columns), grad.dtype)] * inner,
        name="up_pack",
    )(at, *[grad] * inner)


def qkv_pack_kernel(seq_parts, rows, lanes, at_ref, *refs):
    count = len(refs) // 3
    for qkv_ref, out_grad_ref, packed_ref in zip(refs[:count], refs[count : 2 * count], refs[2 * count :]):
        for near in range(seq_parts):
            for c in range(3):
                packed_ref[0, c * rows : (c + 1) * rows, near * lanes : (near + 1) * lanes] = qkv_ref[
                    0, near, :, c * lanes : (c + 1) * lanes
                ]
        packed_ref[0, 3 * rows :, :] = out_grad_ref[0]


def qkv_pack(grad_qkv, grad_out, pair, at):
    dp_parts, seq_parts, rows, columns = grad_qkv.shape
    lanes = columns // 3
    inner = inner_of(dp_parts)
    outer = dp_parts // inner

    def source(j, m, at):
        return at[0] ^ (m * inner + j)

    return pl.pallas_call(
        functools.partial(qkv_pack_kernel, seq_parts, rows, lanes),
        grid_spec=pltpu.PrefetchScalarGridSpec(
            num_scalar_prefetch=1,
            grid=(outer,),
            in_specs=[
                pl.BlockSpec(
                    (1, seq_parts, rows, columns),
                    functools.partial(lambda j, m, at: (source(j, m, at), 0, 0, 0), j),
                )
                for j in range(inner)
            ]
            + [
                pl.BlockSpec(
                    (1, rows, seq_parts * lanes),
                    functools.partial(lambda j, m, at: (source(j, m, at), 0, pair), j),
                )
                for j in range(inner)
            ],
            out_specs=[
                pl.BlockSpec((1, 4 * rows, seq_parts * lanes), lambda m, at: (m, 0, 0))
            ] * inner,
        ),
        out_shape=[
            jax.ShapeDtypeStruct((outer, 4 * rows, seq_parts * lanes), grad_qkv.dtype)
        ] * inner,
        name="qkv_pack",
    )(at, *[grad_qkv] * inner, *[grad_out] * inner)


def qkv_sum_kernel(count, rows, lanes, at_ref, *refs):
    ins, outs = refs[:count], refs[count:]
    total = ins[0][...].astype(jnp.float32)
    for ref in ins[1:]:
        total = total + ref[...].astype(jnp.float32)
    outs[-1][...] = total[3 * rows :].astype(jnp.bfloat16)
    total = total.astype(jnp.bfloat16)
    for t in range(len(outs) - 1):
        for k, out_ref in enumerate(outs[:-1]):

            @pl.when((at_ref[1] ^ k) == t)
            def _():
                out_ref[...] = total[: 3 * rows, t * lanes : (t + 1) * lanes]


def qkv_sum(terms, seq_parts, at):
    all_rows, columns = terms[0].shape
    rows, lanes = all_rows // 4, columns // seq_parts
    full = pl.BlockSpec(memory_space=pltpu.VMEM)
    return pl.pallas_call(
        functools.partial(qkv_sum_kernel, len(terms), rows, lanes),
        in_specs=[pl.BlockSpec(memory_space=pltpu.SMEM)] + [full] * len(terms),
        out_specs=[full] * (seq_parts + 1),
        out_shape=[jax.ShapeDtypeStruct((3 * rows, lanes), jnp.bfloat16)] * seq_parts
        + [jax.ShapeDtypeStruct((rows, columns), jnp.bfloat16)],
        name="qkv_sum",
    )(at, *terms)


def qkv_finish_kernel(pairs, seq_parts, rows, lanes, at_ref, *refs):
    out_ref = refs[-1]
    width = pairs * lanes
    for p in range(pairs):
        for k in range(seq_parts):
            ref = refs[p * seq_parts + k]
            for c in range(3):
                to = (c * seq_parts + (at_ref[1] ^ k)) * width + p * lanes
                out_ref[:, pl.ds(pl.multiple_of(to, lanes), lanes)] = ref[
                    c * rows : (c + 1) * rows, :
                ].astype(jnp.float32)


def qkv_finish(pieces, seq_parts, at):
    pairs = len(pieces)
    rows, lanes = pieces[0][0].shape[0] // 3, pieces[0][0].shape[1]
    full = pl.BlockSpec(memory_space=pltpu.VMEM)
    return pl.pallas_call(
        functools.partial(qkv_finish_kernel, pairs, seq_parts, rows, lanes),
        in_specs=[pl.BlockSpec(memory_space=pltpu.SMEM)] + [full] * (pairs * seq_parts),
        out_specs=full,
        out_shape=jax.ShapeDtypeStruct((rows, 3 * seq_parts * pairs * lanes), jnp.float32),
        name="qkv_finish",
    )(at, *[piece for pair in pieces for piece in pair])


def token_grad_kernel(inner, permute, dp_parts, units, at_ref, *refs):
    lefts, (near_ref, rest_ref), outs = refs[: 2 * inner], refs[2 * inner : 2 * inner + 2], refs[2 * inner + 2 :]
    for j, out_ref in enumerate(outs):
        grad = dot_first(lefts[2 * j][...], near_ref[...])
        grad = (grad + dot_first(lefts[2 * j + 1][...], rest_ref[...])).astype(out_ref.dtype)
        if permute:
            for m, mask in enumerate(mask_order(dp_parts)):
                lanes = pl.ds(pl.multiple_of((at_ref[0] ^ mask) * units, units), units)
                out_ref[0, :, lanes] = grad[:, m * units : (m + 1) * units]
        else:
            out_ref[0] = grad


def token_grad(left, right, permute, dp_parts, units, at):
    inner = inner_of(dp_parts)
    outer = dp_parts // inner
    width = left[0].shape[1] // dp_parts
    columns = right[0].shape[1]
    if width % 128 != 0 or units % 128 != 0:
        grad = jnp.dot(
            jnp.concatenate(left).T, jnp.concatenate(right), preferred_element_type=jnp.float32
        )
        grad = grad.astype(jnp.bfloat16).reshape(dp_parts, width, columns)
        if permute:
            return up_pack(grad, units, at)
        return [grad[j * outer : (j + 1) * outer] for j in range(inner)]

    def source(j, m, at):
        return (0, (at[0] ^ (m * inner + j)) if permute else j * outer + m)

    return pl.pallas_call(
        functools.partial(token_grad_kernel, inner, permute, dp_parts, units),
        grid_spec=pltpu.PrefetchScalarGridSpec(
            num_scalar_prefetch=1,
            grid=(outer,),
            in_specs=[
                pl.BlockSpec((part.shape[0], width), functools.partial(source, j))
                for j in range(inner)
                for part in left
            ]
            + [pl.BlockSpec(part.shape, lambda m, at: (0, 0)) for part in right],
            out_specs=[pl.BlockSpec((1, width, columns), lambda m, at: (m, 0, 0))] * inner,
        ),
        out_shape=[jax.ShapeDtypeStruct((outer, width, columns), jnp.bfloat16)] * inner,
        cost_estimate=pl.CostEstimate(
            flops=2 * sum(p.size for p in left) * columns,
            bytes_accessed=2 * (sum(p.size for p in left) + sum(p.size for p in right) + dp_parts * width * columns),
            transcendentals=0,
        ),
        name="token_grad",
    )(at, *[part for _ in range(inner) for part in left], *right)


def qkv_grad_kernel(inner, seq_parts, rows, lanes, at_ref, *refs):
    lefts, right_ref = refs[:inner], refs[inner]
    outs_in, packs = refs[inner + 1 : 2 * inner + 1], refs[2 * inner + 1 :]
    for left_ref, out_grad_ref, packed_ref in zip(lefts, outs_in, packs):
        grad = dot_first(left_ref[...], right_ref[...]).astype(packed_ref.dtype)
        for near in range(seq_parts):
            for c in range(3):
                packed_ref[0, c * rows : (c + 1) * rows, near * lanes : (near + 1) * lanes] = grad[
                    near * rows : (near + 1) * rows, c * lanes : (c + 1) * lanes
                ]
        packed_ref[0, 3 * rows :, :] = out_grad_ref[0]


def qkv_grad(normed, qkv_half, grad_out, pair, seq_parts, at):
    dp_parts, rows, _ = grad_out.shape
    inner = inner_of(dp_parts)
    outer = dp_parts // inner
    width = seq_parts * rows
    columns = qkv_half.shape[1]
    lanes = columns // 3
    if width % 128 != 0:
        grad = jnp.dot(normed.T, qkv_half, preferred_element_type=jnp.float32)
        grad = grad.astype(jnp.bfloat16).reshape(dp_parts, seq_parts, rows, columns)
        return qkv_pack(grad, grad_out, pair, at)

    def source(j, m, at):
        return at[0] ^ (m * inner + j)

    return pl.pallas_call(
        functools.partial(qkv_grad_kernel, inner, seq_parts, rows, lanes),
        grid_spec=pltpu.PrefetchScalarGridSpec(
            num_scalar_prefetch=1,
            grid=(outer,),
            in_specs=[
                pl.BlockSpec(
                    (normed.shape[0], width),
                    functools.partial(lambda j, m, at: (0, source(j, m, at)), j),
                )
                for j in range(inner)
            ]
            + [pl.BlockSpec(qkv_half.shape, lambda m, at: (0, 0))]
            + [
                pl.BlockSpec(
                    (1, rows, seq_parts * lanes),
                    functools.partial(lambda j, m, at: (source(j, m, at), 0, pair), j),
                )
                for j in range(inner)
            ],
            out_specs=[
                pl.BlockSpec((1, 4 * rows, seq_parts * lanes), lambda m, at: (m, 0, 0))
            ] * inner,
        ),
        out_shape=[
            jax.ShapeDtypeStruct((outer, 4 * rows, seq_parts * lanes), jnp.bfloat16)
        ] * inner,
        cost_estimate=pl.CostEstimate(
            flops=2 * normed.size * columns,
            bytes_accessed=2 * (normed.size + qkv_half.size + dp_parts * 4 * rows * seq_parts * lanes),
            transcendentals=0,
        ),
        name="qkv_grad",
    )(at, *[normed] * inner, qkv_half, *[grad_out] * inner)


def project_kernel(
    width, x_ref, gain_ref, bias_ref, w_ref, qb_ref, vb_ref, n_ref, q_ref, k_ref, v_ref
):
    values = x_ref[...].astype(jnp.float32)
    center = jnp.mean(values, axis=-1, keepdims=True)
    offset = values - center
    spread = jnp.mean(offset * offset, axis=-1, keepdims=True)
    unit = offset * lax.rsqrt(spread + EPSILON)
    normed = (unit * gain_ref[...] + bias_ref[...]).astype(jnp.bfloat16)
    n_ref[...] = normed
    projected = jnp.dot(normed, w_ref[...], preferred_element_type=jnp.float32)
    lanes = pair_width(width)
    for p in range(width // lanes):
        to = slice(p * lanes, (p + 1) * lanes)
        query, key, value = (
            projected[:, (p * 3 + c) * lanes : (p * 3 + c + 1) * lanes] for c in range(3)
        )
        q_ref[:, to] = (query + qb_ref[:, to]).astype(jnp.bfloat16)
        k_ref[:, to] = key.astype(jnp.bfloat16)
        v_ref[:, to] = (value + vb_ref[:, to]).astype(jnp.bfloat16)


def project(tokens, gain, bias, weight, query_part, value_part):
    rows, depth = tokens.shape
    width = weight.shape[1] // 3
    tile = min(256, rows)
    half = jnp.bfloat16

    def whole(shape):
        return pl.BlockSpec(shape, lambda i: (0, 0))

    return pl.pallas_call(
        functools.partial(project_kernel, width),
        grid=(rows // tile,),
        in_specs=[
            pl.BlockSpec((tile, depth), lambda i: (i, 0)),
            whole((1, depth)),
            whole((1, depth)),
            whole((depth, 3 * width)),
            whole((1, width)),
            whole((1, width)),
        ],
        out_specs=[pl.BlockSpec((tile, depth), lambda i: (i, 0))]
        + [pl.BlockSpec((tile, width), lambda i: (i, 0))] * 3,
        out_shape=[jax.ShapeDtypeStruct((rows, depth), half)]
        + [jax.ShapeDtypeStruct((rows, width), half)] * 3,
        name="project",
    )(tokens, gain[None], bias[None], weight, query_part[None], value_part[None])


def head_lanes(width, head):
    lane = lax.broadcasted_iota(jnp.int32, (1, width), 1)
    return (lane // HEAD_DIM) == head


def dot_rows(a, b):
    return lax.dot_general(a, b, (((1,), (1,)), ((), ())), preferred_element_type=jnp.float32)


def dot_first(a, b):
    return lax.dot_general(a, b, (((0,), (0,)), ((), ())), preferred_element_type=jnp.float32)


def attend_kernel(parts, tile, at_ref, seg_col, seg_row, q_ref, k_ref, v_ref, o_ref, lse_ref):
    head = pl.program_id(0)
    seq_me = at_ref[1]
    width = q_ref.shape[1]
    mine = head_lanes(width, head)
    half = jnp.bfloat16

    def rows(i):
        return pl.ds(pl.multiple_of((seq_me ^ i) * tile, tile), tile)

    for i in range(parts):
        q = jnp.where(mine, q_ref[rows(i), :] * SCORE_SCALE, 0).astype(half)
        own = seg_col[i * tile : (i + 1) * tile, :]
        scores = []
        for j in range(i + 1):
            s = dot_rows(q, k_ref[rows(j), :])
            seen = own == seg_row[:, j * tile : (j + 1) * tile]
            if j == i:
                at = lax.broadcasted_iota(jnp.int32, (tile, tile), 0)
                seen = seen & (lax.broadcasted_iota(jnp.int32, (tile, tile), 1) <= at)
            scores.append(jnp.where(seen, s, -jnp.inf))
        top = scores[i].max(axis=-1, keepdims=True)
        for j in range(i):
            top = jnp.maximum(top, scores[j].max(axis=-1, keepdims=True))
        weights = [jnp.exp(s - top) for s in scores]
        total = weights[0].sum(axis=-1, keepdims=True)
        for w in weights[1:]:
            total = total + w.sum(axis=-1, keepdims=True)
        scale = 1.0 / total
        out = None
        for j in range(i + 1):
            term = jnp.dot(
                (weights[j] * scale).astype(half), v_ref[rows(j), :],
                preferred_element_type=jnp.float32,
            )
            out = term if out is None else out + term
        out = out.astype(half)
        before = o_ref[rows(i), :]
        o_ref[rows(i), :] = jnp.where(mine, out, before)
        log_total = jnp.broadcast_to(top + jnp.log(total), (tile, 128)).T
        lse_ref[0, :, i * tile : (i + 1) * tile] = log_total[:8]


def attend(queries, keys, values, segments, at, seq_parts):
    full_len, width = queries.shape
    tile = full_len // seq_parts
    heads = width // HEAD_DIM

    def whole(shape):
        return pl.BlockSpec(shape, lambda h, at: (0,) * len(shape))

    return pl.pallas_call(
        functools.partial(attend_kernel, seq_parts, tile),
        grid_spec=pltpu.PrefetchScalarGridSpec(
            num_scalar_prefetch=1,
            grid=(heads,),
            in_specs=[whole((full_len, 1)), whole((1, full_len))] + [whole((full_len, width))] * 3,
            out_specs=[
                whole((full_len, width)),
                pl.BlockSpec((1, 8, full_len), lambda h, at: (h, 0, 0)),
            ],
        ),
        out_shape=[
            jax.ShapeDtypeStruct((full_len, width), jnp.bfloat16),
            jax.ShapeDtypeStruct((heads, 8, full_len), jnp.float32),
        ],
        name="attend",
    )(at, segments[:, None], segments[None], queries, keys, values)


def attend_back_kernel(
    parts, tile, at_ref, seg_col, seg_row, q_ref, k_ref, v_ref, o_ref, do_ref, lse_ref,
    grad_ref, sum_ref, dq_ref, dk_ref, dv_ref,
):
    head = pl.program_id(0)
    seq_me = at_ref[1]
    width = q_ref.shape[1]
    mine = head_lanes(width, head)
    half = jnp.bfloat16

    @pl.when(head == 0)
    def _():
        dq_ref[...] = jnp.zeros_like(dq_ref)
        dk_ref[...] = jnp.zeros_like(dk_ref)
        dv_ref[...] = jnp.zeros_like(dv_ref)

    def rows(i):
        return pl.ds(pl.multiple_of((seq_me ^ i) * tile, tile), tile)

    for i in range(parts):
        q = jnp.where(mine, q_ref[rows(i), :], 0)
        q_scaled = q * jnp.asarray(SCORE_SCALE, half)
        do = jnp.where(mine, do_ref[rows(i), :], 0)
        own = seg_row[:, i * tile : (i + 1) * tile]
        log_total = lse_ref[0, :1, i * tile : (i + 1) * tile]
        product = do.astype(jnp.float32) * o_ref[rows(i), :].astype(jnp.float32)
        row_dot = jnp.broadcast_to(jnp.sum(product, axis=-1, keepdims=True), (tile, 128)).T[:1]
        dq = None
        for j in range(i + 1):
            k = k_ref[rows(j), :]
            s = dot_rows(k, q_scaled)
            seen = seg_col[j * tile : (j + 1) * tile, :] == own
            if j == i:
                at = lax.broadcasted_iota(jnp.int32, (tile, tile), 0)
                seen = seen & (at <= lax.broadcasted_iota(jnp.int32, (tile, tile), 1))
            prob = jnp.where(seen, jnp.exp(s - log_total), 0.0)
            dv_ref[rows(j), :] += jnp.dot(prob.astype(half), do, preferred_element_type=jnp.float32)
            dp = dot_rows(v_ref[rows(j), :], do)
            ds = (prob * (dp - row_dot) * SCORE_SCALE).astype(half)
            dk_ref[rows(j), :] += jnp.dot(ds, q, preferred_element_type=jnp.float32)
            term = dot_first(ds, k)
            dq = term if dq is None else dq + term
        dq_ref[rows(i), :] += jnp.where(mine, dq, 0.0)

    @pl.when(head == pl.num_programs(0) - 1)
    def _():
        for c, ref in enumerate((dq_ref, dk_ref, dv_ref)):
            value = ref[...]
            grad_ref[:, c * width : (c + 1) * width] = value.astype(half)
            if c != 1:
                spot = 0 if c == 0 else 1
                sum_ref[spot : spot + 1, :] = jnp.sum(value, axis=0, keepdims=True)


def attend_back(pair, queries, keys, values, attended, grads, log_totals, segments, at, seq_parts):
    full_len, width = queries.shape
    tile = full_len // seq_parts
    lanes = pair_width(width)
    heads = lanes // HEAD_DIM

    def whole(shape):
        return pl.BlockSpec(shape, lambda h, at: (0,) * len(shape))

    def of_pair():
        return pl.BlockSpec((full_len, lanes), lambda h, at: (0, pair))

    return pl.pallas_call(
        functools.partial(attend_back_kernel, seq_parts, tile),
        grid_spec=pltpu.PrefetchScalarGridSpec(
            num_scalar_prefetch=1,
            grid=(heads,),
            in_specs=[whole((full_len, 1)), whole((1, full_len))]
            + [of_pair() for _ in range(5)]
            + [pl.BlockSpec((1, 8, full_len), lambda h, at: (pair * heads + h, 0, 0))],
            out_specs=[whole((full_len, 3 * lanes)), whole((8, lanes))],
            scratch_shapes=[pltpu.VMEM((full_len, lanes), jnp.float32)] * 3,
        ),
        out_shape=[
            jax.ShapeDtypeStruct((full_len, 3 * lanes), jnp.bfloat16),
            jax.ShapeDtypeStruct((8, lanes), jnp.float32),
        ],
        name="attend_back",
    )(at, segments[:, None], segments[None], queries, keys, values, attended, grads, log_totals)


def per_device(
    inputs,
    segments,
    ln1_gain,
    ln1_bias,
    qkv_weight,
    query_bias,
    value_bias,
    out_weight,
    out_bias,
    ln2_gain,
    ln2_bias,
    up_weight,
    up_bias,
    down_weight,
    down_bias,
    cotangent,
):
    half = jnp.bfloat16
    wide = jnp.float32
    seq_count, group_len, model_width = inputs.shape
    assert seq_count == 1
    full_len = segments.shape[1]
    dp_parts, seq_parts = lax.axis_size("dp"), lax.axis_size("seq")
    dp_me, seq_me = lax.axis_index("dp"), lax.axis_index("seq")
    at = jnp.stack([dp_me, seq_me]).astype(jnp.int32)
    order = mask_order(dp_parts)
    head_width = model_width // seq_parts
    block = qkv_weight.shape[0]
    down_block = down_weight.shape[0]
    unit_width = dp_parts * down_block
    span = dp_parts // seq_parts

    out_moves = []
    for d in range(dp_parts):
        for s in range(seq_parts):
            source = d * seq_parts + s
            out_moves.append((source, ((d % span) * seq_parts + s) * seq_parts + d // span))

    tokens = inputs.reshape(group_len, model_width)
    pieces = qkv_pieces(
        qkv_weight,
        [
            ln1_gain,
            ln1_bias,
            query_bias,
            value_bias,
            out_bias,
            ln2_gain,
            ln2_bias,
            down_bias,
            up_bias,
        ],
        seq_parts,
        at,
    )
    qkv_mine = jnp.stack(
        [pieces[0]] + [swap(pieces[k], "seq", k) for k in range(1, seq_parts)]
    )
    tokens_far = rows_far(after(tokens, pieces[0]), seq_parts)
    out_chunk = lax.ppermute(out_weight, ("dp", "seq"), out_moves)
    out_outer = gather_outer(out_chunk, dp_parts)
    qkv_outer = gather_outer(qkv_mine, dp_parts)
    up_weight = after(up_weight, qkv_mine)
    pieces = up_pieces(up_weight, dp_parts, seq_parts, at)
    up_mine = jnp.stack([pieces[0]] + [swap(pieces[k], "seq", k) for k in range(1, seq_parts)])
    qkv_groups = gather_inner(qkv_outer, dp_parts)
    qkv_placed, vectors_placed = qkv_place(qkv_groups, block, dp_parts, at)
    qkv_cols = qkv_placed.reshape(model_width, 3 * head_width)
    tokens_full = jnp.concatenate(rows_near(tokens, tokens_far, seq_parts))

    up_outer = gather_outer(after(up_mine, qkv_groups[dp_parts // inner_of(dp_parts)]), dp_parts)
    up_groups = gather_inner(up_outer, dp_parts)
    up_cols = up_place(up_groups, dp_parts, down_block, at).reshape(model_width, unit_width)
    out_part = out_place(gather_inner(out_outer, dp_parts), dp_parts, at)
    out_part = out_part.reshape(head_width, model_width)

    table = vectors_placed.reshape(dp_parts, seq_parts, 3 * head_width)
    (gain_one, bias_one, bias_query, bias_value, bias_out, gain_two, bias_two, bias_down) = (
        table[:, :, i * block : (i + 1) * block].reshape(model_width).astype(wide) for i in range(8)
    )
    bias_up = place_dp(
        lax.dynamic_index_in_dim(table, seq_me, 1, keepdims=False)[
            :, 8 * block : 8 * block + down_block
        ].astype(wide),
        dp_me,
        order,
    ).reshape(unit_width)
    query_part = lax.dynamic_slice_in_dim(bias_query, seq_me * head_width, head_width, 0)
    value_part = lax.dynamic_slice_in_dim(bias_value, seq_me * head_width, head_width, 0)
    upstream = after(cotangent.reshape(group_len, model_width), *tokens_far)
    upstream_near, upstream_rest = rows_near(upstream, rows_far(upstream, seq_parts), seq_parts)

    normed_full, queries, keys_mine, values_mine = project(
        tokens_full, gain_one, bias_one, qkv_cols, query_part, value_part
    )
    down_outer = gather_outer(after(down_weight, queries), dp_parts)
    down_part = jnp.concatenate(gather_inner(down_outer, dp_parts)).reshape(unit_width, model_width)
    attended, log_totals = attend(queries, keys_mine, values_mine, segments[0], at, seq_parts)
    near = 2 * group_len
    out_far = jnp.dot(attended[near:], out_part, preferred_element_type=wide).astype(half)
    out_near = jnp.dot(
        after(attended[:near], out_far), out_part, preferred_element_type=wide
    ).astype(half)
    hidden_in = tokens.astype(wide)
    residual_one = hidden_in + rows_out(out_near, out_far, seq_parts)[0] + bias_out
    normed_two, unit_two, inverse_two = layer_norm(residual_one, gain_two, bias_two)
    normed_two = normed_two.astype(half)
    normed_two_near, normed_two_rest = rows_near(
        normed_two, rows_far(normed_two, seq_parts), seq_parts
    )

    def feed(normed_rows, upstream_rows):
        preact = jnp.dot(normed_rows, up_cols, preferred_element_type=wide) + bias_up
        activated, derivative = gelu_pair(preact)
        preact_grad = jnp.dot(upstream_rows, down_part.T, preferred_element_type=wide) * derivative
        preact_half = preact_grad.astype(half)
        two = jnp.dot(preact_half, up_cols.T, preferred_element_type=wide).astype(half)
        return activated.astype(half), preact_half, two, jnp.sum(preact_grad, axis=0)

    act_near, preact_near, two_near, up_b_near = feed(normed_two_near, upstream_near)
    act_rest, preact_rest, two_rest, up_b_rest = feed(normed_two_rest, upstream_rest)
    grad_up_b = up_b_near + up_b_rest
    normed_two_grad, two_sent = rows_out(two_near, two_rest, seq_parts)

    act_near, act_rest, preact_near, preact_rest = lax.optimization_barrier(
        (act_near, act_rest, preact_near, preact_rest, *two_sent)
    )[:4]
    inner = inner_of(dp_parts)
    grad_down = token_grad(
        (act_near, act_rest), (upstream_near, upstream_rest), False, dp_parts, down_block, at
    )
    down_terms = scatter_outer(scatter_inner(grad_down, dp_parts), dp_parts, half)
    grad_up = token_grad(
        (normed_two_near, normed_two_rest),
        (after(preact_near, grad_down[-1]), preact_rest),
        True,
        dp_parts,
        down_block,
        at,
    )

    upstream_wide = cotangent.astype(wide).reshape(group_len, model_width)
    residual_grad = upstream_wide + layer_norm_back(
        normed_two_grad, unit_two, inverse_two, gain_two
    )
    residual_half = residual_grad.astype(half)
    residual_far = rows_far(residual_half, seq_parts)
    residual_near, residual_rest = rows_near(residual_half, residual_far, seq_parts)
    residual_full = jnp.concatenate([residual_near, residual_rest])
    attended_grad = jnp.concatenate(
        [
            jnp.dot(r, out_part.T, preferred_element_type=wide).astype(half)
            for r in (residual_near, residual_rest)
        ]
    )
    pairs = head_width // pair_width(head_width)
    grad_out = jnp.dot(attended.T, residual_full, preferred_element_type=wide).astype(half)
    grad_out = grad_out.reshape(dp_parts, block, model_width)
    qkv_halves, head_sums, qkv_terms = [], [], []
    for p in range(pairs):
        qkv_half, sums = attend_back(
            p,
            after(queries, *(qkv_terms[-1][0] if p else ())),
            keys_mine,
            values_mine,
            attended,
            attended_grad,
            log_totals,
            segments[0],
            at,
            seq_parts,
        )
        qkv_halves.append(qkv_half)
        head_sums.append(sums)
        packed = qkv_grad(normed_full, qkv_half, grad_out, p, seq_parts, at)
        qkv_terms.append((packed, scatter_inner(packed, dp_parts)))
        if p == 0:
            up_terms = scatter_outer(scatter_inner(grad_up, dp_parts, qkv_half), dp_parts, half)
    qkv_half = after(jnp.concatenate(qkv_halves, axis=1), qkv_terms[-1][0][-1])
    one_far = jnp.dot(qkv_half[near:], qkv_cols.T, preferred_element_type=wide).astype(half)
    one_near = jnp.dot(
        after(qkv_half[:near], one_far), qkv_cols.T, preferred_element_type=wide
    ).astype(half)
    normed_one_grad, one_sent = rows_out(one_near, one_far, seq_parts)
    down_out = [
        jnp.dot(after(a, *one_sent), down_part, preferred_element_type=wide).astype(half)
        for a in (act_near, act_rest)
    ]
    outputs = (residual_one + rows_out(*down_out, seq_parts)[0] + bias_down).astype(half)
    held = lax.optimization_barrier(tuple(down_terms) + tuple(up_terms) + tuple(one_sent))
    down_share = total_of(held[: len(down_terms)])
    up_rows = total_of(held[len(down_terms) : len(down_terms) + len(up_terms)]).astype(half)
    up_rows = up_rows.reshape(seq_parts, block, unit_width)
    up_share = up_finish(
        exchange_seq(
            lambda t: lax.dynamic_index_in_dim(up_rows, t, 0, keepdims=False), seq_me, seq_parts
        ),
        dp_parts,
        seq_parts,
        at,
    )
    _, unit_one, inverse_one = layer_norm(hidden_in, gain_one, bias_one)
    input_grad = residual_grad + layer_norm_back(normed_one_grad, unit_one, inverse_one, gain_one)

    found, out_found = [], []
    for _, part in qkv_terms:
        *columns, out_rows = qkv_sum(scatter_outer(part, dp_parts, half), seq_parts, at)
        found.append([columns[0]] + [swap(columns[k], "seq", k) for k in range(1, seq_parts)])
        out_found.append(lax.ppermute(out_rows, ("dp", "seq"), [(b, a) for a, b in out_moves]))
    qkv_share = qkv_finish(found, seq_parts, at)
    out_share = jnp.concatenate(out_found, axis=1).astype(wide)
    query_sums = jnp.concatenate([sums[0] for sums in head_sums])
    value_sums = jnp.concatenate([sums[1] for sums in head_sums])

    def place_part(part):
        return lax.dynamic_update_slice_in_dim(
            jnp.zeros((model_width,), wide), part, seq_me * head_width, 0
        )

    small = jnp.stack(
        [
            jnp.sum(normed_one_grad * unit_one, axis=0),
            jnp.sum(normed_one_grad, axis=0),
            place_part(query_sums),
            place_part(value_sums),
            jnp.sum(residual_grad, axis=0),
            jnp.sum(normed_two_grad * unit_two, axis=0),
            jnp.sum(normed_two_grad, axis=0),
            jnp.sum(upstream_wide, axis=0),
        ]
    )
    small = small.reshape(8, dp_parts, seq_parts, block).transpose(2, 1, 0, 3)
    small = small.reshape(seq_parts, dp_parts, 8 * block)
    small_mine = sum(
        exchange_seq(
            lambda t: lax.dynamic_index_in_dim(small, t, 0, keepdims=False), seq_me, seq_parts
        )
    )
    small_mine = jnp.concatenate(
        [
            place_dp(small_mine, dp_me, order),
            grad_up_b.reshape(dp_parts, down_block),
        ],
        axis=1,
    ).reshape(inner, dp_parts // inner, -1)
    small_part = scatter_inner([small_mine[j] for j in range(inner)], dp_parts)
    small_total = total_of(scatter_outer(small_part, dp_parts, wide))
    shares = [small_total[i * block : (i + 1) * block] for i in range(8)]
    share_up_b = small_total[8 * block :]

    return (
        outputs[None],
        input_grad[None],
        shares[0],
        shares[1],
        qkv_share,
        shares[2],
        shares[3],
        out_share,
        shares[4],
        shares[5],
        shares[6],
        up_share,
        share_up_b,
        down_share,
        shares[7],
    )


def solution(mesh):
    spread = ("dp", "seq")
    vector, matrix, rows = P(spread), P(spread, None), P("dp", "seq", None)
    return jax.shard_map(
        per_device,
        mesh=mesh,
        in_specs=(
            rows,
            P("dp", None),
            vector,
            vector,
            matrix,
            vector,
            vector,
            matrix,
            vector,
            vector,
            vector,
            matrix,
            vector,
            matrix,
            vector,
            rows,
        ),
        out_specs=(
            rows,
            rows,
            vector,
            vector,
            matrix,
            vector,
            vector,
            matrix,
            vector,
            vector,
            vector,
            matrix,
            vector,
            matrix,
            vector,
        ),
        check_vma=False,
    )
```

```python
import functools

import jax
import jax.numpy as jnp
from jax import lax
from jax.experimental import pallas as pl
from jax.experimental.pallas import tpu as pltpu
from jax.sharding import PartitionSpec as P


HEAD_DIM = 64


EPSILON = 1e-05
SCORE_SCALE = 0.125
GELU_SCALE = 0.7978845608028654
GELU_CUBIC = 0.044715


def layer_norm(values_in, gain_term, bias_term):
    center = jnp.mean(values_in, axis=-1, keepdims=True)
    offset = values_in - center
    spread = jnp.mean(offset * offset, axis=-1, keepdims=True)
    inverse = lax.rsqrt(spread + EPSILON)
    normed = offset * inverse
    return (normed * gain_term.astype(jnp.float32) + bias_term.astype(jnp.float32), normed, inverse)


def layer_norm_back(upstream, normed, inverse, gain_term):
    scaled = upstream * gain_term.astype(jnp.float32)
    mean_grad = jnp.mean(scaled, axis=-1, keepdims=True)
    mean_proj = jnp.mean(scaled * normed, axis=-1, keepdims=True)
    return inverse * (scaled - mean_grad - normed * mean_proj)


def gelu_pair(preact):
    tanh_arg = GELU_SCALE * (preact + GELU_CUBIC * preact * preact * preact)
    tanh_val = jnp.tanh(tanh_arg)
    activated = 0.5 * preact * (1.0 + tanh_val)
    derivative = 0.5 * (1.0 + tanh_val) + 0.5 * preact * (
        1.0 - tanh_val * tanh_val
    ) * GELU_SCALE * (1.0 + 3.0 * GELU_CUBIC * preact * preact)
    return (activated, derivative)


def swap(tensor, axis, mask):
    count = lax.axis_size(axis)
    return lax.ppermute(tensor, axis, [(i, i ^ mask) for i in range(count)])


def inner_of(count):
    inner = 1
    while (inner * 2) ** 2 <= count and count % (inner * 2) == 0:
        inner *= 2
    return inner


def mask_order(count):
    inner = inner_of(count)
    return [k + j for j in range(inner) for k in range(0, count, inner)]


def place_by(pieces, at):
    count = len(pieces)
    stacked = list(pieces)
    bit = 1
    while bit < count:
        flipped = (at & bit) != 0
        stacked = [jnp.where(flipped, stacked[i ^ bit], stacked[i]) for i in range(count)]
        bit *= 2
    return jnp.stack(stacked)


def exchange_seq(piece_for, seq_me, seq_parts):
    return [piece_for(seq_me)] + [
        swap(piece_for(seq_me ^ k), "seq", k) for k in range(1, seq_parts)
    ]


def after(value, *earlier):
    return lax.optimization_barrier((value,) + earlier)[0]


def gather_outer(shard, dp_parts):
    inner = inner_of(dp_parts)
    return [shard] + [swap(shard, "dp", k) for k in range(inner, dp_parts, inner)]


def gather_inner(outer, dp_parts):
    inner = inner_of(dp_parts)
    cut = max(1, len(outer) // 2)
    groups = [b[None] for b in outer]
    if cut < len(outer):
        sends = [jnp.stack(outer[:cut]), jnp.stack(outer[cut:])]
    else:
        sends = [outer[0][None]]
    for j in range(1, inner):
        groups += [swap(s, "dp", j) for s in sends]
    return groups


def scatter_inner(blocks, dp_parts, *earlier):
    part = blocks[0].astype(jnp.float32)
    for j in range(1, inner_of(dp_parts)):
        came = swap(blocks[j], "dp", j)
        if earlier:
            came = after(came, *earlier)
        part = part + came.astype(jnp.float32)
    return part


def scatter_outer(part, dp_parts, dtype):
    inner = inner_of(dp_parts)
    sent = part.astype(dtype)
    return [part[0]] + [swap(sent[k], "dp", k * inner) for k in range(1, dp_parts // inner)]


def total_of(terms):
    total = terms[0]
    for term in terms[1:]:
        total = total + term.astype(jnp.float32)
    return total


def rows_far(tensor, seq_parts):
    return [swap(tensor, "seq", k) for k in range(2, seq_parts, 2)]


def rows_near(tensor, far, seq_parts):
    found = {0: tensor, 1: swap(tensor, "seq", 1)}
    for k in range(2, seq_parts, 2):
        found[k] = far[k // 2 - 1]
        found[k + 1] = swap(found[k], "seq", 1)
    parts = [found[k] for k in range(seq_parts)]
    return jnp.concatenate(parts[:2]), jnp.concatenate(parts[2:]), parts


def rows_out(blocks, seq_parts):
    total, sent = None, []
    for k in reversed(range(0, seq_parts, 2)):
        came = swap(blocks[k + 1], "seq", 1)
        part = blocks[k].astype(jnp.float32) + came.astype(jnp.float32)
        if k:
            sent.append(part.astype(came.dtype))
            part = swap(sent[-1], "seq", k).astype(jnp.float32)
        total = part if total is None else total + part
    return total, sent


def place_dp(rows, dp_me, order):
    found = place_by([rows[i] for i in range(len(order))], dp_me)
    return jnp.stack([found[k] for k in order])


def qkv_place_kernel(sizes, seq_parts, at_ref, *refs):
    ins, main_ref = refs[: len(sizes)], refs[len(sizes)]
    dp_me, seq_me = at_ref[0], at_ref[1]
    order = mask_order(sum(sizes))
    spot = 0
    for ref, size in zip(ins, sizes):
        for g in range(size):
            far = dp_me ^ order[spot]
            for near in range(seq_parts):
                main_ref[far, seq_me ^ near] = ref[g, near]
            spot += 1


def qkv_place(groups, dp_parts, at):
    _, seq_parts, rows, columns = groups[0].shape
    sizes = [g.shape[0] for g in groups]
    wide = 256 if columns % 256 == 0 else columns
    return pl.pallas_call(
        functools.partial(qkv_place_kernel, sizes, seq_parts),
        grid_spec=pltpu.PrefetchScalarGridSpec(
            num_scalar_prefetch=1,
            grid=(columns // wide,),
            in_specs=[
                pl.BlockSpec((size, seq_parts, rows, wide), lambda c, at: (0, 0, 0, c))
                for size in sizes
            ],
            out_specs=pl.BlockSpec((dp_parts, seq_parts, rows, wide), lambda c, at: (0, 0, 0, c)),
        ),
        out_shape=jax.ShapeDtypeStruct((dp_parts, seq_parts, rows, columns), groups[0].dtype),
        name="qkv_place",
    )(at, *groups)


def out_place_kernel(sizes, rows, at_ref, *refs):
    ins, (out_ref, extra_ref) = refs[: len(sizes)], refs[len(sizes) :]
    order = mask_order(sum(sizes))
    spot = 0
    for ref, size in zip(ins, sizes):
        for g in range(size):
            out_ref[at_ref[0] ^ order[spot]] = ref[g, :rows]
            extra_ref[at_ref[0] ^ order[spot]] = ref[g, rows:].astype(jnp.float32)
            spot += 1


def out_place(groups, rows, dp_parts, at):
    _, _, columns = groups[0].shape
    full = pl.BlockSpec(memory_space=pltpu.VMEM)
    return pl.pallas_call(
        functools.partial(out_place_kernel, [g.shape[0] for g in groups], rows),
        in_specs=[pl.BlockSpec(memory_space=pltpu.SMEM)] + [full] * len(groups),
        out_specs=[full] * 2,
        out_shape=[
            jax.ShapeDtypeStruct((dp_parts, rows, columns), groups[0].dtype),
            jax.ShapeDtypeStruct((dp_parts, 1, columns), jnp.float32),
        ],
        name="out_place",
    )(at, *groups)


def join_kernel(*refs):
    spot = 0
    for ref in refs[:-1]:
        refs[-1][spot : spot + ref.shape[0]] = ref[...]
        spot += ref.shape[0]


def join(groups):
    total = sum(g.shape[0] for g in groups)
    rest = groups[0].shape[1:]
    wide = 256 if rest[-1] % 256 == 0 else rest[-1]

    def spec(count):
        return pl.BlockSpec((count,) + rest[:-1] + (wide,), lambda c: (0,) * len(rest) + (c,))

    return pl.pallas_call(
        join_kernel,
        grid=(rest[-1] // wide,),
        in_specs=[spec(g.shape[0]) for g in groups],
        out_specs=spec(total),
        out_shape=jax.ShapeDtypeStruct((total,) + rest, groups[0].dtype),
        name="join",
    )(*groups)


def up_place_kernel(sizes, seq_parts, units, at_ref, *refs):
    ins, up_ref = refs[: len(sizes)], refs[len(sizes)]
    dp_me, seq_me = at_ref[0], at_ref[1]
    order = mask_order(sum(sizes))
    spot = 0
    for ref, size in zip(ins, sizes):
        for g in range(size):
            far = dp_me ^ order[spot]
            for near in range(seq_parts):
                for m, mask in enumerate(order):
                    lanes = pl.ds(pl.multiple_of((dp_me ^ mask) * units, units), units)
                    up_ref[far, seq_me ^ near, :, m * units : (m + 1) * units] = ref[
                        g, near, :, lanes
                    ]
            spot += 1


def up_place(groups, dp_parts, units, at):
    _, seq_parts, rows, columns = groups[0].shape
    sizes = [g.shape[0] for g in groups]
    half = groups[0].dtype
    if units % 128 != 0:
        order = jnp.array(mask_order(dp_parts), jnp.int32)
        both = jnp.concatenate(groups)[jnp.argsort(order ^ at[0])]
        up = both[:, jnp.arange(seq_parts) ^ at[1]]
        up = up.reshape(dp_parts, seq_parts, rows, dp_parts, units)[:, :, :, order ^ at[0]]
        return up.reshape(dp_parts, seq_parts, rows, columns)
    return pl.pallas_call(
        functools.partial(up_place_kernel, sizes, seq_parts, units),
        grid_spec=pltpu.PrefetchScalarGridSpec(
            num_scalar_prefetch=1,
            grid=(1,),
            in_specs=[
                pl.BlockSpec((size, seq_parts, rows, columns), lambda c, at: (0, 0, 0, 0))
                for size in sizes
            ],
            out_specs=pl.BlockSpec(
                (dp_parts, seq_parts, rows, columns), lambda c, at: (0, 0, 0, 0)
            ),
        ),
        out_shape=jax.ShapeDtypeStruct((dp_parts, seq_parts, rows, columns), half),
        name="up_place",
    )(at, *groups)


def pair_width(width):
    return min(128, width)


def qkv_pieces_kernel(depth, width, at_ref, w_ref, *outs):
    lanes = pair_width(width)
    for k, out_ref in enumerate(outs):
        t = at_ref[1] ^ k
        for p in range(width // lanes):
            for c in range(3):
                source = pl.multiple_of(c * depth + t * width + p * lanes, lanes)
                to = (p * 3 + c) * lanes
                out_ref[:, to : to + lanes] = w_ref[:, pl.ds(source, lanes)]


def qkv_pieces(weight, seq_parts, at):
    rows, columns = weight.shape
    depth = columns // 3
    width = depth // seq_parts
    full = pl.BlockSpec(memory_space=pltpu.VMEM)
    return pl.pallas_call(
        functools.partial(qkv_pieces_kernel, depth, width),
        in_specs=[pl.BlockSpec(memory_space=pltpu.SMEM), full],
        out_specs=[full] * seq_parts,
        out_shape=[jax.ShapeDtypeStruct((rows, 3 * width), weight.dtype)] * seq_parts,
        name="qkv_pieces",
    )(at, weight)


def vector_row_kernel(rows, out_w_ref, *refs):
    vectors, out_ref = refs[:-1], refs[-1]
    out_ref[:rows, :] = out_w_ref[...]
    out_ref[rows:, :] = jnp.zeros((1, out_ref.shape[1]), out_ref.dtype)
    spot = 0
    for ref in vectors:
        out_ref[rows:, spot : spot + ref.shape[1]] = ref[...]
        spot += ref.shape[1]


def vector_row(chunk, vectors):
    rows, columns = chunk.shape
    full = pl.BlockSpec(memory_space=pltpu.VMEM)
    return pl.pallas_call(
        functools.partial(vector_row_kernel, rows),
        in_specs=[full] * (1 + len(vectors)),
        out_specs=full,
        out_shape=jax.ShapeDtypeStruct((rows + 1, columns), chunk.dtype),
        name="vector_row",
    )(chunk, *[v[None] for v in vectors])


def up_pieces_kernel(seq_parts, dp_parts, units, at_ref, w_ref, *outs):
    for k, out_ref in enumerate(outs):
        t = at_ref[1] ^ k
        for d in range(dp_parts):
            source = pl.multiple_of((d * seq_parts + t) * units, units)
            out_ref[:, d * units : (d + 1) * units] = w_ref[:, pl.ds(source, units)]


def up_pieces(weight, dp_parts, seq_parts, at):
    rows, columns = weight.shape
    units = columns // (dp_parts * seq_parts)
    width = dp_parts * units
    if units % 128 != 0:
        view = weight.reshape(rows, dp_parts, seq_parts, units)
        return [
            lax.dynamic_index_in_dim(view, at[1] ^ k, 2, keepdims=False).reshape(rows, width)
            for k in range(seq_parts)
        ]
    full = pl.BlockSpec(memory_space=pltpu.VMEM)
    return pl.pallas_call(
        functools.partial(up_pieces_kernel, seq_parts, dp_parts, units),
        in_specs=[pl.BlockSpec(memory_space=pltpu.SMEM), full],
        out_specs=[full] * seq_parts,
        out_shape=[jax.ShapeDtypeStruct((rows, width), weight.dtype)] * seq_parts,
        name="up_pieces",
    )(at, weight)


def up_finish_kernel(dp_parts, seq_parts, units, at_ref, *refs):
    out_ref = refs[-1]
    for k, ref in enumerate(refs[:-1]):
        for d in range(dp_parts):
            to = pl.multiple_of((d * seq_parts + (at_ref[1] ^ k)) * units, units)
            out_ref[:, pl.ds(to, units)] = ref[:, d * units : (d + 1) * units].astype(jnp.float32)


def up_finish(pieces, dp_parts, seq_parts, at):
    rows, width = pieces[0].shape
    units = width // dp_parts
    if units % 128 != 0:
        found = place_by(pieces, at[1]).reshape(seq_parts, rows, dp_parts, units)
        return found.transpose(1, 2, 0, 3).reshape(rows, seq_parts * width).astype(jnp.float32)
    full = pl.BlockSpec(memory_space=pltpu.VMEM)
    return pl.pallas_call(
        functools.partial(up_finish_kernel, dp_parts, seq_parts, units),
        in_specs=[pl.BlockSpec(memory_space=pltpu.SMEM)] + [full] * seq_parts,
        out_specs=full,
        out_shape=jax.ShapeDtypeStruct((rows, seq_parts * width), jnp.float32),
        name="up_finish",
    )(at, *pieces)


def up_pack_kernel(dp_parts, units, at_ref, *refs):
    ins, outs = refs[: len(refs) // 2], refs[len(refs) // 2 :]
    for in_ref, out_ref in zip(ins, outs):
        for m, mask in enumerate(mask_order(dp_parts)):
            lanes = pl.ds(pl.multiple_of((at_ref[0] ^ mask) * units, units), units)
            out_ref[0, :, lanes] = in_ref[0, :, m * units : (m + 1) * units]


def up_pack(grad, units, at):
    dp_parts, rows, columns = grad.shape
    inner = inner_of(dp_parts)
    outer = dp_parts // inner
    if units % 128 != 0:
        order = jnp.array(mask_order(dp_parts), jnp.int32)
        grad = grad[order ^ at[0]].reshape(dp_parts, rows, dp_parts, units)
        grad = grad[:, :, jnp.argsort(order ^ at[0])].reshape(dp_parts, rows, columns)
        return [grad[j * outer : (j + 1) * outer] for j in range(inner)]
    return pl.pallas_call(
        functools.partial(up_pack_kernel, dp_parts, units),
        grid_spec=pltpu.PrefetchScalarGridSpec(
            num_scalar_prefetch=1,
            grid=(outer,),
            in_specs=[
                pl.BlockSpec(
                    (1, rows, columns), functools.partial(lambda j, m, at: (at[0] ^ (m * inner + j), 0, 0), j)
                )
                for j in range(inner)
            ],
            out_specs=[pl.BlockSpec((1, rows, columns), lambda m, at: (m, 0, 0))] * inner,
        ),
        out_shape=[jax.ShapeDtypeStruct((outer, rows, columns), grad.dtype)] * inner,
        name="up_pack",
    )(at, *[grad] * inner)


def qkv_pack_kernel(seq_parts, rows, lanes, at_ref, *refs):
    count = len(refs) // 3
    for qkv_ref, out_grad_ref, packed_ref in zip(refs[:count], refs[count : 2 * count], refs[2 * count :]):
        for near in range(seq_parts):
            for c in range(3):
                packed_ref[0, c * rows : (c + 1) * rows, near * lanes : (near + 1) * lanes] = qkv_ref[
                    0, near, :, c * lanes : (c + 1) * lanes
                ]
        packed_ref[0, 3 * rows :, :] = out_grad_ref[0]


def qkv_pack(grad_qkv, grad_out, pair, at):
    dp_parts, seq_parts, rows, columns = grad_qkv.shape
    lanes = columns // 3
    inner = inner_of(dp_parts)
    outer = dp_parts // inner

    def source(j, m, at):
        return at[0] ^ (m * inner + j)

    return pl.pallas_call(
        functools.partial(qkv_pack_kernel, seq_parts, rows, lanes),
        grid_spec=pltpu.PrefetchScalarGridSpec(
            num_scalar_prefetch=1,
            grid=(outer,),
            in_specs=[
                pl.BlockSpec(
                    (1, seq_parts, rows, columns),
                    functools.partial(lambda j, m, at: (source(j, m, at), 0, 0, 0), j),
                )
                for j in range(inner)
            ]
            + [
                pl.BlockSpec(
                    (1, rows, seq_parts * lanes),
                    functools.partial(lambda j, m, at: (source(j, m, at), 0, pair), j),
                )
                for j in range(inner)
            ],
            out_specs=[
                pl.BlockSpec((1, 4 * rows, seq_parts * lanes), lambda m, at: (m, 0, 0))
            ] * inner,
        ),
        out_shape=[
            jax.ShapeDtypeStruct((outer, 4 * rows, seq_parts * lanes), grad_qkv.dtype)
        ] * inner,
        name="qkv_pack",
    )(at, *[grad_qkv] * inner, *[grad_out] * inner)


def qkv_sum_kernel(pairs, count, rows, lanes, at_ref, *refs):
    ins, outs = refs[: pairs * count], refs[pairs * count :]
    for p in range(pairs):
        total = ins[p * count][...].astype(jnp.float32)
        for ref in ins[p * count + 1 : (p + 1) * count]:
            total = total + ref[...].astype(jnp.float32)
        total = total.astype(jnp.bfloat16)
        width = total.shape[1]
        outs[-1][:, p * width : (p + 1) * width] = total[3 * rows :]
        for t in range(len(outs) - 1):
            for k, out_ref in enumerate(outs[:-1]):

                @pl.when((at_ref[1] ^ k) == t)
                def _():
                    out_ref[:, p * lanes : (p + 1) * lanes] = total[
                        : 3 * rows, t * lanes : (t + 1) * lanes
                    ]


def qkv_sum(terms, seq_parts, at):
    pairs, count = len(terms), len(terms[0])
    all_rows, columns = terms[0][0].shape
    rows, lanes = all_rows // 4, columns // seq_parts
    full = pl.BlockSpec(memory_space=pltpu.VMEM)
    return pl.pallas_call(
        functools.partial(qkv_sum_kernel, pairs, count, rows, lanes),
        in_specs=[pl.BlockSpec(memory_space=pltpu.SMEM)] + [full] * (pairs * count),
        out_specs=[full] * (seq_parts + 1),
        out_shape=[jax.ShapeDtypeStruct((3 * rows, pairs * lanes), jnp.bfloat16)] * seq_parts
        + [jax.ShapeDtypeStruct((rows, pairs * columns), jnp.bfloat16)],
        name="qkv_sum",
    )(at, *[term for pair in terms for term in pair])


def qkv_finish_kernel(seq_parts, rows, width, at_ref, *refs):
    out_ref = refs[-1]
    for k, ref in enumerate(refs[:-1]):
        for c in range(3):
            to = (c * seq_parts + (at_ref[1] ^ k)) * width
            out_ref[:, pl.ds(pl.multiple_of(to, width), width)] = ref[
                c * rows : (c + 1) * rows, :
            ].astype(jnp.float32)


def qkv_finish(pieces, at):
    seq_parts = len(pieces)
    rows, width = pieces[0].shape[0] // 3, pieces[0].shape[1]
    full = pl.BlockSpec(memory_space=pltpu.VMEM)
    return pl.pallas_call(
        functools.partial(qkv_finish_kernel, seq_parts, rows, width),
        in_specs=[pl.BlockSpec(memory_space=pltpu.SMEM)] + [full] * seq_parts,
        out_specs=full,
        out_shape=jax.ShapeDtypeStruct((rows, 3 * seq_parts * width), jnp.float32),
        name="qkv_finish",
    )(at, *pieces)


def tiles_of(refs, tile):
    return [(ref, i) for ref in refs for i in range(0, ref.shape[0], tile)]


def token_grad_kernel(inner, left_count, permute, dp_parts, units, at_ref, *refs):
    lefts = refs[: inner * left_count]
    outs = refs[len(refs) - inner :]
    rights = refs[inner * left_count : len(refs) - inner]
    tile = min(ref.shape[0] for ref in (*lefts, *rights))
    rights = tiles_of(rights, tile)
    columns = [tiles_of(lefts[j * left_count : (j + 1) * left_count], tile) for j in range(inner)]
    grad = None
    for spot, (right_ref, row) in enumerate(rights):
        left = jnp.concatenate([c[spot][0][c[spot][1] : c[spot][1] + tile, :] for c in columns], 1)
        term = dot_first(left, right_ref[row : row + tile, :])
        grad = term if grad is None else grad + term
    width = grad.shape[0] // inner
    for j, out_ref in enumerate(outs):
        mine = grad[j * width : (j + 1) * width].astype(out_ref.dtype)
        if permute:
            for m, mask in enumerate(mask_order(dp_parts)):
                lanes = pl.ds(pl.multiple_of((at_ref[0] ^ mask) * units, units), units)
                out_ref[0, :, lanes] = mine[:, m * units : (m + 1) * units]
        else:
            out_ref[0] = mine


def token_grad(left, right, permute, dp_parts, units, at):
    inner = inner_of(dp_parts)
    outer = dp_parts // inner
    width = left[0].shape[1] // dp_parts
    columns = right[0].shape[1]
    if width % 128 != 0 or units % 128 != 0:
        grad = jnp.dot(
            jnp.concatenate(left).T, jnp.concatenate(right), preferred_element_type=jnp.float32
        )
        grad = grad.astype(jnp.bfloat16).reshape(dp_parts, width, columns)
        if permute:
            return up_pack(grad, units, at)
        return [grad[j * outer : (j + 1) * outer] for j in range(inner)]

    def source(j, m, at):
        return (0, (at[0] ^ (m * inner + j)) if permute else j * outer + m)

    sizes = sum(p.size for p in left), sum(p.size for p in right), dp_parts * width * columns
    return pl.pallas_call(
        functools.partial(token_grad_kernel, inner, len(left), permute, dp_parts, units),
        grid_spec=pltpu.PrefetchScalarGridSpec(
            num_scalar_prefetch=1,
            grid=(outer,),
            in_specs=[
                pl.BlockSpec((part.shape[0], width), functools.partial(source, j))
                for j in range(inner)
                for part in left
            ]
            + [pl.BlockSpec(part.shape, lambda m, at: (0, 0)) for part in right],
            out_specs=[pl.BlockSpec((1, width, columns), lambda m, at: (m, 0, 0))] * inner,
        ),
        out_shape=[jax.ShapeDtypeStruct((outer, width, columns), jnp.bfloat16)] * inner,
        cost_estimate=pl.CostEstimate(
            flops=2 * sizes[0] * columns, bytes_accessed=2 * sum(sizes), transcendentals=0
        ),
        name="token_grad",
    )(at, *[part for _ in range(inner) for part in left], *right)


def qkv_grad_kernel(inner, seq_parts, rows, lanes, at_ref, *refs):
    lefts, right_ref = refs[:inner], refs[inner]
    outs_in, packs = refs[inner + 1 : 2 * inner + 1], refs[2 * inner + 1 :]
    both = dot_first(jnp.concatenate([ref[...] for ref in lefts], 1), right_ref[...])
    both = both.astype(packs[0].dtype)
    width = seq_parts * rows
    for j, (out_grad_ref, packed_ref) in enumerate(zip(outs_in, packs)):
        grad = both[j * width : (j + 1) * width]
        for near in range(seq_parts):
            for c in range(3):
                packed_ref[0, c * rows : (c + 1) * rows, near * lanes : (near + 1) * lanes] = grad[
                    near * rows : (near + 1) * rows, c * lanes : (c + 1) * lanes
                ]
        packed_ref[0, 3 * rows :, :] = out_grad_ref[0]


def qkv_grad(normed, qkv_half, grad_out, pair, seq_parts, at):
    dp_parts, rows, _ = grad_out.shape
    inner = inner_of(dp_parts)
    outer = dp_parts // inner
    width = seq_parts * rows
    columns = qkv_half.shape[1] // (pair + 1)
    lanes = columns // 3
    if width % 128 != 0:
        mine = qkv_half[:, pair * columns :]
        grad = jnp.dot(normed.T, mine, preferred_element_type=jnp.float32)
        grad = grad.astype(jnp.bfloat16).reshape(dp_parts, seq_parts, rows, columns)
        return qkv_pack(grad, grad_out, pair, at)

    def source(j, m, at):
        return at[0] ^ (m * inner + j)

    return pl.pallas_call(
        functools.partial(qkv_grad_kernel, inner, seq_parts, rows, lanes),
        grid_spec=pltpu.PrefetchScalarGridSpec(
            num_scalar_prefetch=1,
            grid=(outer,),
            in_specs=[
                pl.BlockSpec(
                    (normed.shape[0], width),
                    functools.partial(lambda j, m, at: (0, source(j, m, at)), j),
                )
                for j in range(inner)
            ]
            + [pl.BlockSpec((qkv_half.shape[0], columns), lambda m, at: (0, pair))]
            + [
                pl.BlockSpec(
                    (1, rows, seq_parts * lanes),
                    functools.partial(lambda j, m, at: (source(j, m, at), 0, pair), j),
                )
                for j in range(inner)
            ],
            out_specs=[
                pl.BlockSpec((1, 4 * rows, seq_parts * lanes), lambda m, at: (m, 0, 0))
            ] * inner,
        ),
        out_shape=[
            jax.ShapeDtypeStruct((outer, 4 * rows, seq_parts * lanes), jnp.bfloat16)
        ] * inner,
        cost_estimate=pl.CostEstimate(
            flops=2 * normed.size * columns,
            bytes_accessed=2 * (normed.size + qkv_half.size + dp_parts * 4 * rows * seq_parts * lanes),
            transcendentals=0,
        ),
        name="qkv_grad",
    )(at, *[normed] * inner, qkv_half, *[grad_out] * inner)


def project_kernel(
    width, count, *refs
):
    parts = refs[:count]
    gain_ref, bias_ref, w_ref, qb_ref, vb_ref, n_ref, q_ref, k_ref, v_ref, x_ref = refs[count:]
    for k, part_ref in enumerate(parts):

        @pl.when(pl.program_id(0) == k)
        def _():
            x_ref[...] = part_ref[...]

    values = x_ref[...].astype(jnp.float32)
    center = jnp.mean(values, axis=-1, keepdims=True)
    offset = values - center
    spread = jnp.mean(offset * offset, axis=-1, keepdims=True)
    unit = offset * lax.rsqrt(spread + EPSILON)
    normed = (unit * gain_ref[...] + bias_ref[...]).astype(jnp.bfloat16)
    n_ref[...] = normed
    projected = jnp.dot(normed, w_ref[...], preferred_element_type=jnp.float32)
    lanes = pair_width(width)
    for p in range(width // lanes):
        to = slice(p * lanes, (p + 1) * lanes)
        query, key, value = (
            projected[:, (p * 3 + c) * lanes : (p * 3 + c + 1) * lanes] for c in range(3)
        )
        q_ref[:, to] = (query + qb_ref[:, to]).astype(jnp.bfloat16)
        k_ref[:, to] = key.astype(jnp.bfloat16)
        v_ref[:, to] = (value + vb_ref[:, to]).astype(jnp.bfloat16)


def project(tokens, gain, bias, weight, query_part, value_part):
    tile, depth = tokens[0].shape
    rows = tile * len(tokens)
    width = weight.shape[1] // 3
    half = jnp.bfloat16

    def whole(shape):
        return pl.BlockSpec(shape, lambda i: (0, 0))

    return pl.pallas_call(
        functools.partial(project_kernel, width, len(tokens)),
        grid=(len(tokens),),
        in_specs=[whole((tile, depth)) for _ in tokens]
        + [
            whole((1, depth)),
            whole((1, depth)),
            whole((depth, 3 * width)),
            whole((1, width)),
            whole((1, width)),
        ],
        out_specs=[pl.BlockSpec((tile, depth), lambda i: (i, 0))]
        + [pl.BlockSpec((tile, width), lambda i: (i, 0))] * 3,
        out_shape=[jax.ShapeDtypeStruct((rows, depth), half)]
        + [jax.ShapeDtypeStruct((rows, width), half)] * 3,
        scratch_shapes=[pltpu.VMEM((tile, depth), half)],
        cost_estimate=pl.CostEstimate(
            flops=6 * rows * depth * width, bytes_accessed=8 * rows * depth, transcendentals=0
        ),
        name="project",
    )(*tokens, gain[None], bias[None], weight, query_part[None], value_part[None])


def head_lanes(width, head):
    lane = lax.broadcasted_iota(jnp.int32, (1, width), 1)
    return (lane // HEAD_DIM) == head


def dot_rows(a, b):
    return lax.dot_general(a, b, (((1,), (1,)), ((), ())), preferred_element_type=jnp.float32)


def dot_first(a, b):
    return lax.dot_general(a, b, (((0,), (0,)), ((), ())), preferred_element_type=jnp.float32)


def attend_kernel(pair, parts, tile, at_ref, seg_col, seg_row, q_ref, k_ref, v_ref, *refs):
    before_ref = refs[0] if pair else None
    o_ref, lse_ref = refs[-2:]
    head = pl.program_id(0)
    seq_me = at_ref[1]
    width = q_ref.shape[1]
    mine = head_lanes(width, head)
    half = jnp.bfloat16
    lanes = slice(pair * width, (pair + 1) * width)

    if pair:

        @pl.when(head == 0)
        def _():
            o_ref[:, : pair * width] = before_ref[...]

    def rows(i):
        return pl.ds(pl.multiple_of((seq_me ^ i) * tile, tile), tile)

    for i in range(parts):
        q = jnp.where(mine, q_ref[rows(i), :] * SCORE_SCALE, 0).astype(half)
        own = seg_col[i * tile : (i + 1) * tile, :]
        scores = []
        for j in range(i + 1):
            s = dot_rows(q, k_ref[rows(j), :])
            seen = own == seg_row[:, j * tile : (j + 1) * tile]
            if j == i:
                at = lax.broadcasted_iota(jnp.int32, (tile, tile), 0)
                seen = seen & (lax.broadcasted_iota(jnp.int32, (tile, tile), 1) <= at)
            scores.append(jnp.where(seen, s, -jnp.inf))
        top = scores[i].max(axis=-1, keepdims=True)
        for j in range(i):
            top = jnp.maximum(top, scores[j].max(axis=-1, keepdims=True))
        weights = [jnp.exp(s - top) for s in scores]
        total = weights[0].sum(axis=-1, keepdims=True)
        for w in weights[1:]:
            total = total + w.sum(axis=-1, keepdims=True)
        scale = 1.0 / total
        out = None
        for j in range(i + 1):
            term = jnp.dot(
                (weights[j] * scale).astype(half), v_ref[rows(j), :],
                preferred_element_type=jnp.float32,
            )
            out = term if out is None else out + term
        out = out.astype(half)
        o_ref[rows(i), lanes] = jnp.where(mine, out, o_ref[rows(i), lanes])
        log_total = jnp.broadcast_to(top + jnp.log(total), (tile, 128)).T
        lse_ref[0, :, i * tile : (i + 1) * tile] = log_total[:8]


def attend(pair, before, queries, keys, values, segments, at, seq_parts):
    full_len, width = queries.shape
    tile = full_len // seq_parts
    lanes = pair_width(width)
    heads = lanes // HEAD_DIM

    def whole(shape):
        return pl.BlockSpec(shape, lambda h, at: (0,) * len(shape))

    return pl.pallas_call(
        functools.partial(attend_kernel, pair, seq_parts, tile),
        grid_spec=pltpu.PrefetchScalarGridSpec(
            num_scalar_prefetch=1,
            grid=(heads,),
            in_specs=[whole((full_len, 1)), whole((1, full_len))]
            + [pl.BlockSpec((full_len, lanes), lambda h, at: (0, pair)) for _ in range(3)]
            + [whole(b.shape) for b in before],
            out_specs=[
                whole((full_len, (pair + 1) * lanes)),
                pl.BlockSpec((1, 8, full_len), lambda h, at: (h, 0, 0)),
            ],
        ),
        out_shape=[
            jax.ShapeDtypeStruct((full_len, (pair + 1) * lanes), jnp.bfloat16),
            jax.ShapeDtypeStruct((heads, 8, full_len), jnp.float32),
        ],
        cost_estimate=pl.CostEstimate(
            flops=8 * full_len * full_len * lanes,
            bytes_accessed=8 * full_len * lanes,
            transcendentals=full_len * full_len * heads // 2,
        ),
        name="attend",
    )(at, segments[:, None], segments[None], queries, keys, values, *before)


def one_term_kernel(tile, *refs):
    left_ref, weight_ref, outs = refs[0], refs[1], refs[2:]
    for k, out_ref in enumerate(outs):
        rows = slice(k * tile, (k + 1) * tile)
        out_ref[...] = dot_rows(left_ref[rows, :], weight_ref[...]).astype(out_ref.dtype)


def one_term(part, count, left, weight, tile):
    columns, depth = weight.shape
    return pl.pallas_call(
        functools.partial(one_term_kernel, tile),
        grid=(1,),
        in_specs=[
            pl.BlockSpec((count * tile, depth), lambda i: (part, 0)),
            pl.BlockSpec((columns, depth), lambda i: (0, 0)),
        ],
        out_specs=[pl.BlockSpec((tile, columns), lambda i: (0, 0))] * count,
        out_shape=[jax.ShapeDtypeStruct((tile, columns), jnp.bfloat16)] * count,
        cost_estimate=pl.CostEstimate(
            flops=2 * count * tile * columns * depth,
            bytes_accessed=2 * columns * depth,
            transcendentals=0,
        ),
        name="one_term",
    )(left, weight)


def attend_back_kernel(
    pair, parts, tile, at_ref, seg_col, seg_row, q_ref, k_ref, v_ref, o_ref, do_ref, lse_ref, *refs
):
    before_ref = refs[0] if pair else None
    grad_ref, sum_ref, dq_ref, dk_ref, dv_ref = refs[-5:]
    head = pl.program_id(0)
    seq_me = at_ref[1]
    width = q_ref.shape[1]
    mine = head_lanes(width, head)
    half = jnp.bfloat16

    @pl.when(head == 0)
    def _():
        dq_ref[...] = jnp.zeros_like(dq_ref)
        dk_ref[...] = jnp.zeros_like(dk_ref)
        dv_ref[...] = jnp.zeros_like(dv_ref)
        if pair:
            grad_ref[:, : 3 * pair * width] = before_ref[...]

    def rows(i):
        return pl.ds(pl.multiple_of((seq_me ^ i) * tile, tile), tile)

    for i in range(parts):
        q = jnp.where(mine, q_ref[rows(i), :], 0)
        q_scaled = q * jnp.asarray(SCORE_SCALE, half)
        do = jnp.where(mine, do_ref[rows(i), :], 0)
        own = seg_row[:, i * tile : (i + 1) * tile]
        log_total = lse_ref[0, :1, i * tile : (i + 1) * tile]
        product = do.astype(jnp.float32) * o_ref[rows(i), :].astype(jnp.float32)
        row_dot = jnp.broadcast_to(jnp.sum(product, axis=-1, keepdims=True), (tile, 128)).T[:1]
        dq = None
        for j in range(i + 1):
            k = k_ref[rows(j), :]
            s = dot_rows(k, q_scaled)
            seen = seg_col[j * tile : (j + 1) * tile, :] == own
            if j == i:
                at = lax.broadcasted_iota(jnp.int32, (tile, tile), 0)
                seen = seen & (at <= lax.broadcasted_iota(jnp.int32, (tile, tile), 1))
            prob = jnp.where(seen, jnp.exp(s - log_total), 0.0)
            dv_ref[rows(j), :] += jnp.dot(prob.astype(half), do, preferred_element_type=jnp.float32)
            dp = dot_rows(v_ref[rows(j), :], do)
            ds = (prob * (dp - row_dot) * SCORE_SCALE).astype(half)
            dk_ref[rows(j), :] += jnp.dot(ds, q, preferred_element_type=jnp.float32)
            term = dot_first(ds, k)
            dq = term if dq is None else dq + term
        dq_ref[rows(i), :] += jnp.where(mine, dq, 0.0)

    @pl.when(head == pl.num_programs(0) - 1)
    def _():
        for c, ref in enumerate((dq_ref, dk_ref, dv_ref)):
            value = ref[...]
            to = (3 * pair + c) * width
            grad_ref[:, to : to + width] = value.astype(half)
            if c != 1:
                spot = 0 if c == 0 else 1
                sum_ref[spot : spot + 1, :] = jnp.sum(value, axis=0, keepdims=True)


def attend_back(
    pair, before, queries, keys, values, attended, grads, log_totals, segments, at, seq_parts
):
    full_len, width = queries.shape
    tile = full_len // seq_parts
    lanes = pair_width(width)
    heads = lanes // HEAD_DIM

    def whole(shape):
        return pl.BlockSpec(shape, lambda h, at: (0,) * len(shape))

    def of_pair():
        return pl.BlockSpec((full_len, lanes), lambda h, at: (0, pair))

    return pl.pallas_call(
        functools.partial(attend_back_kernel, pair, seq_parts, tile),
        grid_spec=pltpu.PrefetchScalarGridSpec(
            num_scalar_prefetch=1,
            grid=(heads,),
            in_specs=[whole((full_len, 1)), whole((1, full_len))]
            + [of_pair() for _ in range(5)]
            + [pl.BlockSpec((1, 8, full_len), lambda h, at: (h, 0, 0))]
            + [whole(b.shape) for b in before],
            out_specs=[whole((full_len, 3 * (pair + 1) * lanes)), whole((8, lanes))],
            scratch_shapes=[pltpu.VMEM((full_len, lanes), jnp.float32)] * 3,
        ),
        out_shape=[
            jax.ShapeDtypeStruct((full_len, 3 * (pair + 1) * lanes), jnp.bfloat16),
            jax.ShapeDtypeStruct((8, lanes), jnp.float32),
        ],
        cost_estimate=pl.CostEstimate(
            flops=20 * full_len * full_len * lanes,
            bytes_accessed=16 * full_len * lanes,
            transcendentals=full_len * full_len * heads // 2,
        ),
        name="attend_back",
    )(
        at, segments[:, None], segments[None], queries, keys, values, attended, grads, log_totals,
        *before,
    )


def per_device(
    inputs,
    segments,
    ln1_gain,
    ln1_bias,
    qkv_weight,
    query_bias,
    value_bias,
    out_weight,
    out_bias,
    ln2_gain,
    ln2_bias,
    up_weight,
    up_bias,
    down_weight,
    down_bias,
    cotangent,
):
    half = jnp.bfloat16
    wide = jnp.float32
    seq_count, group_len, model_width = inputs.shape
    assert seq_count == 1
    dp_parts, seq_parts = lax.axis_size("dp"), lax.axis_size("seq")
    dp_me, seq_me = lax.axis_index("dp"), lax.axis_index("seq")
    at = jnp.stack([dp_me, seq_me]).astype(jnp.int32)
    order = mask_order(dp_parts)
    head_width = model_width // seq_parts
    block = qkv_weight.shape[0]
    down_block = down_weight.shape[0]
    unit_width = dp_parts * down_block
    span = dp_parts // seq_parts

    out_moves = []
    for d in range(dp_parts):
        for s in range(seq_parts):
            source = d * seq_parts + s
            out_moves.append((source, ((d % span) * seq_parts + s) * seq_parts + d // span))

    tokens = inputs.reshape(group_len, model_width)
    pieces = qkv_pieces(qkv_weight, seq_parts, at)
    qkv_mine = jnp.stack([pieces[0]] + [swap(pieces[k], "seq", k) for k in range(1, seq_parts)])
    tokens_far = rows_far(tokens, seq_parts)
    out_moved = lax.ppermute(out_weight, ("dp", "seq"), out_moves)
    out_chunk = vector_row(
        out_moved,
        [
            ln1_gain,
            ln1_bias,
            query_bias,
            value_bias,
            out_bias,
            ln2_gain,
            ln2_bias,
            down_bias,
            up_bias,
        ],
    )
    out_outer = gather_outer(out_chunk, dp_parts)
    qkv_outer = gather_outer(qkv_mine, dp_parts)
    pieces = up_pieces(up_weight, dp_parts, seq_parts, at)
    up_mine = jnp.stack([pieces[0]] + [swap(pieces[k], "seq", k) for k in range(1, seq_parts)])
    qkv_groups = gather_inner(qkv_outer, dp_parts)
    qkv_cols = qkv_place(qkv_groups, dp_parts, at).reshape(model_width, 3 * head_width)
    tokens_parts = rows_near(tokens, tokens_far, seq_parts)[2]

    out_part, vectors = out_place(gather_inner(out_outer, dp_parts), block, dp_parts, at)
    out_part = out_part.reshape(head_width, model_width)
    vectors = vectors[:, 0, : 8 * block + down_block]
    bias_up = place_dp(vectors[:, 8 * block :], dp_me, order).reshape(unit_width)
    vectors = vectors[:, : 8 * block].astype(half)
    table = place_by(
        [vectors] + [swap(vectors, "seq", k) for k in range(1, seq_parts)], seq_me
    ).astype(wide)
    table = table.reshape(seq_parts, dp_parts, 8, block).transpose(2, 1, 0, 3)
    table = table.reshape(8, model_width)
    (gain_one, bias_one, bias_query, bias_value, bias_out, gain_two, bias_two, bias_down) = (
        table[i] for i in range(8)
    )

    up_outer = gather_outer(up_mine, dp_parts)
    query_part = lax.dynamic_slice_in_dim(bias_query, seq_me * head_width, head_width, 0)
    value_part = lax.dynamic_slice_in_dim(bias_value, seq_me * head_width, head_width, 0)
    upstream = cotangent.reshape(group_len, model_width)
    upstream_near, upstream_rest, upstream_parts = rows_near(
        upstream, rows_far(upstream, seq_parts), seq_parts
    )

    normed_full, queries, keys_mine, values_mine = project(
        tokens_parts, gain_one, bias_one, qkv_cols, query_part, value_part
    )
    up_groups = gather_inner(up_outer, dp_parts)
    up_cols = up_place(up_groups, dp_parts, down_block, at).reshape(model_width, unit_width)
    down_outer = gather_outer(down_weight, dp_parts)
    down_part = join(gather_inner(down_outer, dp_parts)).reshape(unit_width, model_width)
    pairs = head_width // pair_width(head_width)
    before, log_totals = [], []
    for p in range(pairs):
        attended, log_total = attend(
            p, before, queries, keys_mine, values_mine, segments[0], at, seq_parts
        )
        before = [attended]
        log_totals.append(log_total)

    def block_dots(rows, weight):
        found = [None] * seq_parts
        for k in reversed(range(seq_parts)):
            found[k] = jnp.dot(
                rows[k * group_len : (k + 1) * group_len], weight, preferred_element_type=wide
            ).astype(half)
        return found

    hidden_in = tokens.astype(wide)
    attended_sum = rows_out(block_dots(attended, out_part), seq_parts)[0]
    residual_one = hidden_in + attended_sum + bias_out
    normed_two, unit_two, inverse_two = layer_norm(residual_one, gain_two, bias_two)
    normed_two = normed_two.astype(half)
    normed_two_near, normed_two_rest, normed_two_parts = rows_near(
        normed_two, rows_far(normed_two, seq_parts), seq_parts
    )

    def feed(normed_rows, upstream_rows):
        preact = jnp.dot(normed_rows, up_cols, preferred_element_type=wide) + bias_up
        activated, derivative = gelu_pair(preact)
        preact_grad = jnp.dot(upstream_rows, down_part.T, preferred_element_type=wide) * derivative
        preact_half = preact_grad.astype(half)
        two = [
            jnp.dot(
                preact_half[i : i + group_len], up_cols.T, preferred_element_type=wide
            ).astype(half)
            for i in range(0, preact_half.shape[0], group_len)
        ]
        return activated.astype(half), preact_half, two, jnp.sum(preact_grad, axis=0)

    act_near, preact_near, two_near, up_b_near = feed(normed_two_near, upstream_near)
    act_rest, preact_rest, two_rest, up_b_rest = feed(normed_two_rest, upstream_rest)
    grad_up_b = up_b_near + up_b_rest
    normed_two_grad, two_sent = rows_out(two_near + two_rest, seq_parts)

    act_near, act_rest, preact_near, preact_rest = lax.optimization_barrier(
        (act_near, act_rest, preact_near, preact_rest, *two_sent)
    )[:4]
    inner = inner_of(dp_parts)
    grad_down = token_grad((act_near, act_rest), upstream_parts, False, dp_parts, down_block, at)
    down_terms = scatter_outer(scatter_inner(grad_down, dp_parts), dp_parts, half)
    grad_up = token_grad(
        normed_two_parts,
        (after(preact_near, grad_down[-1]), preact_rest),
        True,
        dp_parts,
        down_block,
        at,
    )

    upstream_wide = cotangent.astype(wide).reshape(group_len, model_width)
    residual_grad = upstream_wide + layer_norm_back(
        normed_two_grad, unit_two, inverse_two, gain_two
    )
    residual_half = residual_grad.astype(half)
    residual_far = rows_far(residual_half, seq_parts)
    residual_near, residual_rest, _ = rows_near(residual_half, residual_far, seq_parts)
    residual_full = jnp.concatenate([residual_near, residual_rest])
    attended_grad = jnp.concatenate(
        [
            jnp.dot(r, out_part.T, preferred_element_type=wide).astype(half)
            for r in (residual_near, residual_rest)
        ]
    )
    grad_out = jnp.dot(attended.T, residual_full, preferred_element_type=wide).astype(half)
    grad_out = grad_out.reshape(dp_parts, block, model_width)
    before, head_sums, qkv_terms, earlier = [], [], [], []
    for p in range(pairs):
        qkv_half, sums = attend_back(
            p,
            before,
            after(queries, *earlier),
            keys_mine,
            values_mine,
            attended,
            attended_grad,
            log_totals[p],
            segments[0],
            at,
            seq_parts,
        )
        before = [qkv_half]
        head_sums.append(sums)
        packed = qkv_grad(normed_full, qkv_half, grad_out, p, seq_parts, at)
        qkv_terms.append((packed, scatter_inner(packed, dp_parts)))
        earlier = packed
        if p == 0:
            up_part = scatter_inner(grad_up, dp_parts, qkv_half)
            up_terms = scatter_outer(up_part, dp_parts, half)
    one_blocks = []
    for part in (0, 1):
        count = seq_parts - 2 if part else 2
        if seq_parts == 4:
            one_blocks += one_term(part, count, qkv_half, qkv_cols, group_len)
        else:
            one_blocks += [
                jnp.dot(
                    qkv_half[k * group_len : (k + 1) * group_len],
                    qkv_cols.T,
                    preferred_element_type=wide,
                ).astype(half)
                for k in (range(2, seq_parts) if part else range(2))
            ]
    normed_one_grad, _ = rows_out(one_blocks, seq_parts)
    down_out = [
        jnp.dot(
            after(a, up_part)[i : i + group_len], down_part, preferred_element_type=wide
        ).astype(half)
        for a in (act_near, act_rest)
        for i in range(0, a.shape[0], group_len)
    ]
    down_sum = rows_out(down_out, seq_parts)[0]
    outputs = (residual_one + down_sum + bias_down).astype(half)
    _, unit_one, inverse_one = layer_norm(hidden_in, gain_one, bias_one)
    input_grad = residual_grad + layer_norm_back(normed_one_grad, unit_one, inverse_one, gain_one)

    query_sums = jnp.concatenate([sums[0] for sums in head_sums])
    value_sums = jnp.concatenate([sums[1] for sums in head_sums])

    def place_part(part):
        return lax.dynamic_update_slice_in_dim(
            jnp.zeros((model_width,), wide), part, seq_me * head_width, 0
        )

    early = jnp.stack(
        [
            place_part(query_sums),
            place_part(value_sums),
            jnp.sum(residual_grad, axis=0),
            jnp.sum(normed_two_grad * unit_two, axis=0),
            jnp.sum(normed_two_grad, axis=0),
            jnp.sum(upstream_wide, axis=0),
        ]
    )
    late = jnp.stack(
        [jnp.sum(normed_one_grad * unit_one, axis=0), jnp.sum(normed_one_grad, axis=0)]
    )
    found = [None] * dp_parts
    for m, mask in enumerate(order):
        found[mask] = grad_up_b.reshape(dp_parts, down_block)[m]
    grad_up_b = place_by(found, dp_me).reshape(1, unit_width)
    grad_up_b = jnp.pad(grad_up_b, ((0, 0), (0, model_width - unit_width)))

    def add_over(small, axis, parts):
        mask = 1
        while mask < parts:
            small = small + swap(small, axis, mask)
            mask *= 2
        return small

    small = add_over(jnp.concatenate([late, early]), "seq", seq_parts)
    small = add_over(jnp.concatenate([small, grad_up_b]), "dp", dp_parts)

    terms = [scatter_outer(part, dp_parts, half) for _, part in qkv_terms]
    *columns, out_rows = qkv_sum(terms, seq_parts, at)
    found = [columns[0]] + [swap(columns[k], "seq", k) for k in range(1, seq_parts)]
    out_share = lax.ppermute(out_rows, ("dp", "seq"), [(b, a) for a, b in out_moves]).astype(wide)
    qkv_share = qkv_finish(found, at)
    down_share = total_of(down_terms)
    up_rows = total_of(up_terms).astype(half)
    up_rows = up_rows.reshape(seq_parts, block, unit_width)
    up_share = up_finish(
        exchange_seq(
            lambda t: lax.dynamic_index_in_dim(up_rows, t, 0, keepdims=False), seq_me, seq_parts
        ),
        dp_parts,
        seq_parts,
        at,
    )
    spot = (dp_me * seq_parts + seq_me) * block
    own = lax.dynamic_slice_in_dim(small[:8], spot, block, 1)
    shares = [own[i] for i in range(8)]
    share_up_b = lax.dynamic_slice_in_dim(small[8], dp_me * down_block, down_block, 0)

    return (
        outputs[None],
        input_grad[None],
        shares[0],
        shares[1],
        qkv_share,
        shares[2],
        shares[3],
        out_share,
        shares[4],
        shares[5],
        shares[6],
        up_share,
        share_up_b,
        down_share,
        shares[7],
    )


def solution(mesh):
    spread = ("dp", "seq")
    vector, matrix, rows = P(spread), P(spread, None), P("dp", "seq", None)
    return jax.shard_map(
        per_device,
        mesh=mesh,
        in_specs=(
            rows,
            P("dp", None),
            vector,
            vector,
            matrix,
            vector,
            vector,
            matrix,
            vector,
            vector,
            vector,
            matrix,
            vector,
            matrix,
            vector,
            rows,
        ),
        out_specs=(
            rows,
            rows,
            vector,
            vector,
            matrix,
            vector,
            vector,
            matrix,
            vector,
            vector,
            vector,
            matrix,
            vector,
            matrix,
            vector,
        ),
        check_vma=False,
    )
```

```python
import functools

import jax
import jax.numpy as jnp
from jax import lax
from jax.experimental import pallas as pl
from jax.experimental.pallas import tpu as pltpu
from jax.sharding import PartitionSpec as P


HEAD_DIM = 64


EPSILON = 1e-05
SCORE_SCALE = 0.125
GELU_SCALE = 0.7978845608028654
GELU_CUBIC = 0.044715


DP, SEQ = "dp", "seq"


def layer_norm(values_in, gain_term, bias_term):
    center = jnp.mean(values_in, axis=-1, keepdims=True)
    offset = values_in - center
    spread = jnp.mean(offset * offset, axis=-1, keepdims=True)
    inverse = lax.rsqrt(spread + EPSILON)
    normed = offset * inverse
    return (normed * gain_term.astype(jnp.float32) + bias_term.astype(jnp.float32), normed, inverse)


def layer_norm_back(upstream, normed, inverse, gain_term):
    scaled = upstream * gain_term.astype(jnp.float32)
    mean_grad = jnp.mean(scaled, axis=-1, keepdims=True)
    mean_proj = jnp.mean(scaled * normed, axis=-1, keepdims=True)
    return inverse * (scaled - mean_grad - normed * mean_proj)


def gelu_pair(preact):
    tanh_arg = GELU_SCALE * (preact + GELU_CUBIC * preact * preact * preact)
    tanh_val = jnp.tanh(tanh_arg)
    activated = 0.5 * preact * (1.0 + tanh_val)
    derivative = 0.5 * (1.0 + tanh_val) + 0.5 * preact * (
        1.0 - tanh_val * tanh_val
    ) * GELU_SCALE * (1.0 + 3.0 * GELU_CUBIC * preact * preact)
    return (activated, derivative)


def swap(tensor, axis, mask):
    count = lax.axis_size(axis)
    return lax.ppermute(tensor, axis, [(i, i ^ mask) for i in range(count)])


def inner_of(count):
    inner = 1
    while (inner * 2) ** 2 <= count and count % (inner * 2) == 0:
        inner *= 2
    return inner


def mask_order(count):
    inner = inner_of(count)
    return [k + j for j in range(inner) for k in range(0, count, inner)]


def place_by(pieces, at):
    count = len(pieces)
    stacked = list(pieces)
    bit = 1
    while bit < count:
        flipped = (at & bit) != 0
        stacked = [jnp.where(flipped, stacked[i ^ bit], stacked[i]) for i in range(count)]
        bit *= 2
    return jnp.stack(stacked)


def exchange_seq(piece_for, seq_me, seq_parts):
    return [piece_for(seq_me)] + [swap(piece_for(seq_me ^ k), SEQ, k) for k in range(1, seq_parts)]


def after(value, *earlier):
    return lax.optimization_barrier((value,) + earlier)[0]


def gather_outer(shard, dp_parts):
    inner = inner_of(dp_parts)
    return [shard] + [swap(shard, DP, k) for k in range(inner, dp_parts, inner)]


def gather_inner(outer, dp_parts):
    inner = inner_of(dp_parts)
    cut = max(1, len(outer) // 2)
    groups = [b[None] for b in outer]
    if cut < len(outer):
        sends = [jnp.stack(outer[:cut]), jnp.stack(outer[cut:])]
    else:
        sends = [outer[0][None]]
    for j in range(1, inner):
        groups += [swap(s, DP, j) for s in sends]
    return groups


def scatter_inner(blocks, dp_parts, *earlier):
    part = blocks[0].astype(jnp.float32)
    for j in range(1, inner_of(dp_parts)):
        came = swap(blocks[j], DP, j)
        if earlier:
            came = after(came, *earlier)
        part = part + came.astype(jnp.float32)
    return part


def scatter_outer(part, dp_parts, dtype):
    inner = inner_of(dp_parts)
    sent = part.astype(dtype)
    return [part[0]] + [swap(sent[k], DP, k * inner) for k in range(1, dp_parts // inner)]


def total_of(terms):
    total = terms[0]
    for term in terms[1:]:
        total = total + term.astype(jnp.float32)
    return total


def rows_far(tensor, seq_parts):
    return [swap(tensor, SEQ, k) for k in range(2, seq_parts, 2)]


def rows_near(tensor, far, seq_parts):
    found = {0: tensor, 1: swap(tensor, SEQ, 1)}
    for k in range(2, seq_parts, 2):
        found[k] = far[k // 2 - 1]
        found[k + 1] = swap(found[k], SEQ, 1)
    parts = [found[k] for k in range(seq_parts)]
    return jnp.concatenate(parts[:2]), jnp.concatenate(parts[2:]), parts


def rows_out(blocks, seq_parts):
    total, sent = None, []
    for k in reversed(range(0, seq_parts, 2)):
        came = swap(blocks[k + 1], SEQ, 1)
        part = blocks[k].astype(jnp.float32) + came.astype(jnp.float32)
        if k:
            sent.append(part.astype(came.dtype))
            part = swap(sent[-1], SEQ, k).astype(jnp.float32)
        total = part if total is None else total + part
    return total, sent


def place_dp(rows, dp_me, order):
    found = place_by([rows[i] for i in range(len(order))], dp_me)
    return jnp.stack([found[k] for k in order])


def qkv_place_kernel(sizes, seq_parts, at_ref, *refs):
    ins, main_ref = refs[: len(sizes)], refs[len(sizes)]
    dp_me, seq_me = at_ref[0], at_ref[1]
    order = mask_order(sum(sizes))
    spot = 0
    for ref, size in zip(ins, sizes):
        for g in range(size):
            far = dp_me ^ order[spot]
            for near in range(seq_parts):
                main_ref[far, seq_me ^ near] = ref[g, near]
            spot += 1


def qkv_place(groups, dp_parts, at):
    _, seq_parts, rows, columns = groups[0].shape
    sizes = [g.shape[0] for g in groups]
    wide = 256 if columns % 256 == 0 else columns
    return pl.pallas_call(
        functools.partial(qkv_place_kernel, sizes, seq_parts),
        grid_spec=pltpu.PrefetchScalarGridSpec(
            num_scalar_prefetch=1,
            grid=(columns // wide,),
            in_specs=[
                pl.BlockSpec((size, seq_parts, rows, wide), lambda c, at: (0, 0, 0, c))
                for size in sizes
            ],
            out_specs=pl.BlockSpec((dp_parts, seq_parts, rows, wide), lambda c, at: (0, 0, 0, c)),
        ),
        out_shape=jax.ShapeDtypeStruct((dp_parts, seq_parts, rows, columns), groups[0].dtype),
    )(at, *groups)


def out_place_kernel(sizes, rows, at_ref, *refs):
    ins, (out_ref, extra_ref) = refs[: len(sizes)], refs[len(sizes) :]
    order = mask_order(sum(sizes))
    spot = 0
    for ref, size in zip(ins, sizes):
        for g in range(size):
            out_ref[at_ref[0] ^ order[spot]] = ref[g, :rows]
            extra_ref[at_ref[0] ^ order[spot]] = ref[g, rows:].astype(jnp.float32)
            spot += 1


def out_place(groups, rows, dp_parts, at):
    _, _, columns = groups[0].shape
    full = pl.BlockSpec(memory_space=pltpu.VMEM)
    return pl.pallas_call(
        functools.partial(out_place_kernel, [g.shape[0] for g in groups], rows),
        in_specs=[pl.BlockSpec(memory_space=pltpu.SMEM)] + [full] * len(groups),
        out_specs=[full] * 2,
        out_shape=[
            jax.ShapeDtypeStruct((dp_parts, rows, columns), groups[0].dtype),
            jax.ShapeDtypeStruct((dp_parts, 1, columns), jnp.float32),
        ],
    )(at, *groups)


def join_kernel(*refs):
    spot = 0
    for ref in refs[:-1]:
        refs[-1][spot : spot + ref.shape[0]] = ref[...]
        spot += ref.shape[0]


def join(groups):
    total = sum(g.shape[0] for g in groups)
    rest = groups[0].shape[1:]
    wide = 256 if rest[-1] % 256 == 0 else rest[-1]

    def spec(count):
        return pl.BlockSpec((count,) + rest[:-1] + (wide,), lambda c: (0,) * len(rest) + (c,))

    return pl.pallas_call(
        join_kernel,
        grid=(rest[-1] // wide,),
        in_specs=[spec(g.shape[0]) for g in groups],
        out_specs=spec(total),
        out_shape=jax.ShapeDtypeStruct((total,) + rest, groups[0].dtype),
    )(*groups)


def up_place_kernel(sizes, seq_parts, units, at_ref, *refs):
    ins, up_ref = refs[: len(sizes)], refs[len(sizes)]
    dp_me, seq_me = at_ref[0], at_ref[1]
    order = mask_order(sum(sizes))
    spot = 0
    for ref, size in zip(ins, sizes):
        for g in range(size):
            far = dp_me ^ order[spot]
            for near in range(seq_parts):
                for m, mask in enumerate(order):
                    lanes = pl.ds(pl.multiple_of((dp_me ^ mask) * units, units), units)
                    up_ref[far, seq_me ^ near, :, m * units : (m + 1) * units] = ref[
                        g, near, :, lanes
                    ]
            spot += 1


def up_place(groups, dp_parts, units, at):
    _, seq_parts, rows, columns = groups[0].shape
    sizes = [g.shape[0] for g in groups]
    half = groups[0].dtype
    if units % 128 != 0:
        order = jnp.array(mask_order(dp_parts), jnp.int32)
        both = jnp.concatenate(groups)[jnp.argsort(order ^ at[0])]
        up = both[:, jnp.arange(seq_parts) ^ at[1]]
        up = up.reshape(dp_parts, seq_parts, rows, dp_parts, units)[:, :, :, order ^ at[0]]
        return up.reshape(dp_parts, seq_parts, rows, columns)
    return pl.pallas_call(
        functools.partial(up_place_kernel, sizes, seq_parts, units),
        grid_spec=pltpu.PrefetchScalarGridSpec(
            num_scalar_prefetch=1,
            grid=(1,),
            in_specs=[
                pl.BlockSpec((size, seq_parts, rows, columns), lambda c, at: (0, 0, 0, 0))
                for size in sizes
            ],
            out_specs=pl.BlockSpec(
                (dp_parts, seq_parts, rows, columns), lambda c, at: (0, 0, 0, 0)
            ),
        ),
        out_shape=jax.ShapeDtypeStruct((dp_parts, seq_parts, rows, columns), half),
    )(at, *groups)


def pair_width(width):
    return min(128, width)


def qkv_pieces_kernel(depth, width, at_ref, w_ref, *outs):
    lanes = pair_width(width)
    for k, out_ref in enumerate(outs):
        t = at_ref[1] ^ k
        for p in range(width // lanes):
            for c in range(3):
                source = pl.multiple_of(c * depth + t * width + p * lanes, lanes)
                to = (p * 3 + c) * lanes
                out_ref[:, to : to + lanes] = w_ref[:, pl.ds(source, lanes)]


def qkv_pieces(weight, seq_parts, at):
    rows, columns = weight.shape
    depth = columns // 3
    width = depth // seq_parts
    full = pl.BlockSpec(memory_space=pltpu.VMEM)
    return pl.pallas_call(
        functools.partial(qkv_pieces_kernel, depth, width),
        in_specs=[pl.BlockSpec(memory_space=pltpu.SMEM), full],
        out_specs=[full] * seq_parts,
        out_shape=[jax.ShapeDtypeStruct((rows, 3 * width), weight.dtype)] * seq_parts,
    )(at, weight)


def vector_row_kernel(rows, out_w_ref, *refs):
    vectors, out_ref = refs[:-1], refs[-1]
    out_ref[:rows, :] = out_w_ref[...]
    out_ref[rows:, :] = jnp.zeros((1, out_ref.shape[1]), out_ref.dtype)
    spot = 0
    for ref in vectors:
        out_ref[rows:, spot : spot + ref.shape[1]] = ref[...]
        spot += ref.shape[1]


def vector_row(chunk, vectors):
    rows, columns = chunk.shape
    full = pl.BlockSpec(memory_space=pltpu.VMEM)
    return pl.pallas_call(
        functools.partial(vector_row_kernel, rows),
        in_specs=[full] * (1 + len(vectors)),
        out_specs=full,
        out_shape=jax.ShapeDtypeStruct((rows + 1, columns), chunk.dtype),
    )(chunk, *[v[None] for v in vectors])


def up_pieces_kernel(seq_parts, dp_parts, units, at_ref, w_ref, *outs):
    for k, out_ref in enumerate(outs):
        t = at_ref[1] ^ k
        for d in range(dp_parts):
            source = pl.multiple_of((d * seq_parts + t) * units, units)
            out_ref[:, d * units : (d + 1) * units] = w_ref[:, pl.ds(source, units)]


def up_pieces(weight, dp_parts, seq_parts, at):
    rows, columns = weight.shape
    units = columns // (dp_parts * seq_parts)
    width = dp_parts * units
    if units % 128 != 0:
        view = weight.reshape(rows, dp_parts, seq_parts, units)
        return [
            lax.dynamic_index_in_dim(view, at[1] ^ k, 2, keepdims=False).reshape(rows, width)
            for k in range(seq_parts)
        ]
    full = pl.BlockSpec(memory_space=pltpu.VMEM)
    return pl.pallas_call(
        functools.partial(up_pieces_kernel, seq_parts, dp_parts, units),
        in_specs=[pl.BlockSpec(memory_space=pltpu.SMEM), full],
        out_specs=[full] * seq_parts,
        out_shape=[jax.ShapeDtypeStruct((rows, width), weight.dtype)] * seq_parts,
    )(at, weight)


def up_finish_kernel(dp_parts, seq_parts, units, at_ref, *refs):
    out_ref = refs[-1]
    for k, ref in enumerate(refs[:-1]):
        for d in range(dp_parts):
            to = pl.multiple_of((d * seq_parts + (at_ref[1] ^ k)) * units, units)
            out_ref[:, pl.ds(to, units)] = ref[:, d * units : (d + 1) * units].astype(jnp.float32)


def up_finish(pieces, dp_parts, seq_parts, at):
    rows, width = pieces[0].shape
    units = width // dp_parts
    if units % 128 != 0:
        found = place_by(pieces, at[1]).reshape(seq_parts, rows, dp_parts, units)
        return found.transpose(1, 2, 0, 3).reshape(rows, seq_parts * width).astype(jnp.float32)
    full = pl.BlockSpec(memory_space=pltpu.VMEM)
    return pl.pallas_call(
        functools.partial(up_finish_kernel, dp_parts, seq_parts, units),
        in_specs=[pl.BlockSpec(memory_space=pltpu.SMEM)] + [full] * seq_parts,
        out_specs=full,
        out_shape=jax.ShapeDtypeStruct((rows, seq_parts * width), jnp.float32),
    )(at, *pieces)


def up_pack_kernel(dp_parts, units, at_ref, *refs):
    ins, outs = refs[: len(refs) // 2], refs[len(refs) // 2 :]
    for in_ref, out_ref in zip(ins, outs):
        for m, mask in enumerate(mask_order(dp_parts)):
            lanes = pl.ds(pl.multiple_of((at_ref[0] ^ mask) * units, units), units)
            out_ref[0, :, lanes] = in_ref[0, :, m * units : (m + 1) * units]


def up_pack(grad, units, at):
    dp_parts, rows, columns = grad.shape
    inner = inner_of(dp_parts)
    outer = dp_parts // inner
    if units % 128 != 0:
        order = jnp.array(mask_order(dp_parts), jnp.int32)
        grad = grad[order ^ at[0]].reshape(dp_parts, rows, dp_parts, units)
        grad = grad[:, :, jnp.argsort(order ^ at[0])].reshape(dp_parts, rows, columns)
        return [grad[j * outer : (j + 1) * outer] for j in range(inner)]
    return pl.pallas_call(
        functools.partial(up_pack_kernel, dp_parts, units),
        grid_spec=pltpu.PrefetchScalarGridSpec(
            num_scalar_prefetch=1,
            grid=(outer,),
            in_specs=[
                pl.BlockSpec(
                    (1, rows, columns), functools.partial(lambda j, m, at: (at[0] ^ (m * inner + j), 0, 0), j)
                )
                for j in range(inner)
            ],
            out_specs=[pl.BlockSpec((1, rows, columns), lambda m, at: (m, 0, 0))] * inner,
        ),
        out_shape=[jax.ShapeDtypeStruct((outer, rows, columns), grad.dtype)] * inner,
    )(at, *[grad] * inner)


def qkv_pack_kernel(seq_parts, rows, lanes, at_ref, *refs):
    count = len(refs) // 3
    for qkv_ref, out_grad_ref, packed_ref in zip(refs[:count], refs[count : 2 * count], refs[2 * count :]):
        for near in range(seq_parts):
            for c in range(3):
                packed_ref[0, c * rows : (c + 1) * rows, near * lanes : (near + 1) * lanes] = qkv_ref[
                    0, near, :, c * lanes : (c + 1) * lanes
                ]
        packed_ref[0, 3 * rows :, :] = out_grad_ref[0]


def qkv_pack(grad_qkv, grad_out, pair, at):
    dp_parts, seq_parts, rows, columns = grad_qkv.shape
    lanes = columns // 3
    inner = inner_of(dp_parts)
    outer = dp_parts // inner

    def source(j, m, at):
        return at[0] ^ (m * inner + j)

    return pl.pallas_call(
        functools.partial(qkv_pack_kernel, seq_parts, rows, lanes),
        grid_spec=pltpu.PrefetchScalarGridSpec(
            num_scalar_prefetch=1,
            grid=(outer,),
            in_specs=[
                pl.BlockSpec(
                    (1, seq_parts, rows, columns),
                    functools.partial(lambda j, m, at: (source(j, m, at), 0, 0, 0), j),
                )
                for j in range(inner)
            ]
            + [
                pl.BlockSpec(
                    (1, rows, seq_parts * lanes),
                    functools.partial(lambda j, m, at: (source(j, m, at), 0, pair), j),
                )
                for j in range(inner)
            ],
            out_specs=[
                pl.BlockSpec((1, 4 * rows, seq_parts * lanes), lambda m, at: (m, 0, 0))
            ] * inner,
        ),
        out_shape=[
            jax.ShapeDtypeStruct((outer, 4 * rows, seq_parts * lanes), grad_qkv.dtype)
        ] * inner,
    )(at, *[grad_qkv] * inner, *[grad_out] * inner)


def qkv_sum_kernel(pairs, count, rows, lanes, at_ref, *refs):
    ins, outs = refs[: pairs * count], refs[pairs * count :]
    for p in range(pairs):
        total = ins[p * count][...].astype(jnp.float32)
        for ref in ins[p * count + 1 : (p + 1) * count]:
            total = total + ref[...].astype(jnp.float32)
        total = total.astype(jnp.bfloat16)
        width = total.shape[1]
        outs[-1][:, p * width : (p + 1) * width] = total[3 * rows :]
        for t in range(len(outs) - 1):
            for k, out_ref in enumerate(outs[:-1]):

                @pl.when((at_ref[1] ^ k) == t)
                def _():
                    out_ref[:, p * lanes : (p + 1) * lanes] = total[
                        : 3 * rows, t * lanes : (t + 1) * lanes
                    ]


def qkv_sum(terms, seq_parts, at):
    pairs, count = len(terms), len(terms[0])
    all_rows, columns = terms[0][0].shape
    rows, lanes = all_rows // 4, columns // seq_parts
    full = pl.BlockSpec(memory_space=pltpu.VMEM)
    return pl.pallas_call(
        functools.partial(qkv_sum_kernel, pairs, count, rows, lanes),
        in_specs=[pl.BlockSpec(memory_space=pltpu.SMEM)] + [full] * (pairs * count),
        out_specs=[full] * (seq_parts + 1),
        out_shape=[jax.ShapeDtypeStruct((3 * rows, pairs * lanes), jnp.bfloat16)] * seq_parts
        + [jax.ShapeDtypeStruct((rows, pairs * columns), jnp.bfloat16)],
    )(at, *[term for pair in terms for term in pair])


def qkv_finish_kernel(seq_parts, rows, width, at_ref, *refs):
    out_ref = refs[-1]
    for k, ref in enumerate(refs[:-1]):
        for c in range(3):
            to = (c * seq_parts + (at_ref[1] ^ k)) * width
            out_ref[:, pl.ds(pl.multiple_of(to, width), width)] = ref[
                c * rows : (c + 1) * rows, :
            ].astype(jnp.float32)


def qkv_finish(pieces, at):
    seq_parts = len(pieces)
    rows, width = pieces[0].shape[0] // 3, pieces[0].shape[1]
    full = pl.BlockSpec(memory_space=pltpu.VMEM)
    return pl.pallas_call(
        functools.partial(qkv_finish_kernel, seq_parts, rows, width),
        in_specs=[pl.BlockSpec(memory_space=pltpu.SMEM)] + [full] * seq_parts,
        out_specs=full,
        out_shape=jax.ShapeDtypeStruct((rows, 3 * seq_parts * width), jnp.float32),
    )(at, *pieces)


def tiles_of(refs, tile):
    return [(ref, i) for ref in refs for i in range(0, ref.shape[0], tile)]


def token_grad_kernel(inner, left_count, permute, dp_parts, units, at_ref, *refs):
    lefts = refs[: inner * left_count]
    outs = refs[len(refs) - inner :]
    rights = refs[inner * left_count : len(refs) - inner]
    tile = min(ref.shape[0] for ref in (*lefts, *rights))
    rights = tiles_of(rights, tile)
    columns = [tiles_of(lefts[j * left_count : (j + 1) * left_count], tile) for j in range(inner)]
    grad = None
    for spot, (right_ref, row) in enumerate(rights):
        left = jnp.concatenate([c[spot][0][c[spot][1] : c[spot][1] + tile, :] for c in columns], 1)
        term = dot_first(left, right_ref[row : row + tile, :])
        grad = term if grad is None else grad + term
    width = grad.shape[0] // inner
    for j, out_ref in enumerate(outs):
        mine = grad[j * width : (j + 1) * width].astype(out_ref.dtype)
        if permute:
            for m, mask in enumerate(mask_order(dp_parts)):
                lanes = pl.ds(pl.multiple_of((at_ref[0] ^ mask) * units, units), units)
                out_ref[0, :, lanes] = mine[:, m * units : (m + 1) * units]
        else:
            out_ref[0] = mine


def token_grad(left, right, permute, dp_parts, units, at):
    inner = inner_of(dp_parts)
    outer = dp_parts // inner
    width = left[0].shape[1] // dp_parts
    columns = right[0].shape[1]
    if width % 128 != 0 or units % 128 != 0:
        grad = jnp.dot(
            jnp.concatenate(left).T, jnp.concatenate(right), preferred_element_type=jnp.float32
        )
        grad = grad.astype(jnp.bfloat16).reshape(dp_parts, width, columns)
        if permute:
            return up_pack(grad, units, at)
        return [grad[j * outer : (j + 1) * outer] for j in range(inner)]

    def source(j, m, at):
        return (0, (at[0] ^ (m * inner + j)) if permute else j * outer + m)

    sizes = sum(p.size for p in left), sum(p.size for p in right), dp_parts * width * columns
    return pl.pallas_call(
        functools.partial(token_grad_kernel, inner, len(left), permute, dp_parts, units),
        grid_spec=pltpu.PrefetchScalarGridSpec(
            num_scalar_prefetch=1,
            grid=(outer,),
            in_specs=[
                pl.BlockSpec((part.shape[0], width), functools.partial(source, j))
                for j in range(inner)
                for part in left
            ]
            + [pl.BlockSpec(part.shape, lambda m, at: (0, 0)) for part in right],
            out_specs=[pl.BlockSpec((1, width, columns), lambda m, at: (m, 0, 0))] * inner,
        ),
        out_shape=[jax.ShapeDtypeStruct((outer, width, columns), jnp.bfloat16)] * inner,
        cost_estimate=pl.CostEstimate(
            flops=2 * sizes[0] * columns, bytes_accessed=2 * sum(sizes), transcendentals=0
        ),
    )(at, *[part for _ in range(inner) for part in left], *right)


def qkv_grad_kernel(inner, seq_parts, rows, lanes, at_ref, *refs):
    lefts, right_ref = refs[:inner], refs[inner]
    outs_in, packs = refs[inner + 1 : 2 * inner + 1], refs[2 * inner + 1 :]
    both = dot_first(jnp.concatenate([ref[...] for ref in lefts], 1), right_ref[...])
    both = both.astype(packs[0].dtype)
    width = seq_parts * rows
    for j, (out_grad_ref, packed_ref) in enumerate(zip(outs_in, packs)):
        grad = both[j * width : (j + 1) * width]
        for near in range(seq_parts):
            for c in range(3):
                packed_ref[0, c * rows : (c + 1) * rows, near * lanes : (near + 1) * lanes] = grad[
                    near * rows : (near + 1) * rows, c * lanes : (c + 1) * lanes
                ]
        packed_ref[0, 3 * rows :, :] = out_grad_ref[0]


def qkv_grad(normed, qkv_half, grad_out, pair, seq_parts, at):
    dp_parts, rows, _ = grad_out.shape
    inner = inner_of(dp_parts)
    outer = dp_parts // inner
    width = seq_parts * rows
    columns = qkv_half.shape[1] // (pair + 1)
    lanes = columns // 3
    if width % 128 != 0:
        mine = qkv_half[:, pair * columns :]
        grad = jnp.dot(normed.T, mine, preferred_element_type=jnp.float32)
        grad = grad.astype(jnp.bfloat16).reshape(dp_parts, seq_parts, rows, columns)
        return qkv_pack(grad, grad_out, pair, at)

    def source(j, m, at):
        return at[0] ^ (m * inner + j)

    return pl.pallas_call(
        functools.partial(qkv_grad_kernel, inner, seq_parts, rows, lanes),
        grid_spec=pltpu.PrefetchScalarGridSpec(
            num_scalar_prefetch=1,
            grid=(outer,),
            in_specs=[
                pl.BlockSpec(
                    (normed.shape[0], width),
                    functools.partial(lambda j, m, at: (0, source(j, m, at)), j),
                )
                for j in range(inner)
            ]
            + [pl.BlockSpec((qkv_half.shape[0], columns), lambda m, at: (0, pair))]
            + [
                pl.BlockSpec(
                    (1, rows, seq_parts * lanes),
                    functools.partial(lambda j, m, at: (source(j, m, at), 0, pair), j),
                )
                for j in range(inner)
            ],
            out_specs=[
                pl.BlockSpec((1, 4 * rows, seq_parts * lanes), lambda m, at: (m, 0, 0))
            ] * inner,
        ),
        out_shape=[
            jax.ShapeDtypeStruct((outer, 4 * rows, seq_parts * lanes), jnp.bfloat16)
        ] * inner,
        cost_estimate=pl.CostEstimate(
            flops=2 * normed.size * columns,
            bytes_accessed=2 * (normed.size + qkv_half.size + dp_parts * 4 * rows * seq_parts * lanes),
            transcendentals=0,
        ),
    )(at, *[normed] * inner, qkv_half, *[grad_out] * inner)


def project_kernel(
    width, count, *refs
):
    parts = refs[:count]
    gain_ref, bias_ref, w_ref, qb_ref, vb_ref, n_ref, q_ref, k_ref, v_ref, x_ref = refs[count:]
    for k, part_ref in enumerate(parts):

        @pl.when(pl.program_id(0) == k)
        def _():
            x_ref[...] = part_ref[...]

    values = x_ref[...].astype(jnp.float32)
    center = jnp.mean(values, axis=-1, keepdims=True)
    offset = values - center
    spread = jnp.mean(offset * offset, axis=-1, keepdims=True)
    unit = offset * lax.rsqrt(spread + EPSILON)
    normed = (unit * gain_ref[...] + bias_ref[...]).astype(jnp.bfloat16)
    n_ref[...] = normed
    projected = jnp.dot(normed, w_ref[...], preferred_element_type=jnp.float32)
    lanes = pair_width(width)
    for p in range(width // lanes):
        to = slice(p * lanes, (p + 1) * lanes)
        query, key, value = (
            projected[:, (p * 3 + c) * lanes : (p * 3 + c + 1) * lanes] for c in range(3)
        )
        q_ref[:, to] = (query + qb_ref[:, to]).astype(jnp.bfloat16)
        k_ref[:, to] = key.astype(jnp.bfloat16)
        v_ref[:, to] = (value + vb_ref[:, to]).astype(jnp.bfloat16)


def project(tokens, gain, bias, weight, query_part, value_part):
    tile, depth = tokens[0].shape
    rows = tile * len(tokens)
    width = weight.shape[1] // 3
    half = jnp.bfloat16

    def whole(shape):
        return pl.BlockSpec(shape, lambda i: (0, 0))

    return pl.pallas_call(
        functools.partial(project_kernel, width, len(tokens)),
        grid=(len(tokens),),
        in_specs=[whole((tile, depth)) for _ in tokens]
        + [
            whole((1, depth)),
            whole((1, depth)),
            whole((depth, 3 * width)),
            whole((1, width)),
            whole((1, width)),
        ],
        out_specs=[pl.BlockSpec((tile, depth), lambda i: (i, 0))]
        + [pl.BlockSpec((tile, width), lambda i: (i, 0))] * 3,
        out_shape=[jax.ShapeDtypeStruct((rows, depth), half)]
        + [jax.ShapeDtypeStruct((rows, width), half)] * 3,
        scratch_shapes=[pltpu.VMEM((tile, depth), half)],
        cost_estimate=pl.CostEstimate(
            flops=6 * rows * depth * width, bytes_accessed=8 * rows * depth, transcendentals=0
        ),
    )(*tokens, gain[None], bias[None], weight, query_part[None], value_part[None])


def head_lanes(width, head):
    lane = lax.broadcasted_iota(jnp.int32, (1, width), 1)
    return (lane // HEAD_DIM) == head


def dot_rows(a, b):
    return lax.dot_general(a, b, (((1,), (1,)), ((), ())), preferred_element_type=jnp.float32)


def dot_first(a, b):
    return lax.dot_general(a, b, (((0,), (0,)), ((), ())), preferred_element_type=jnp.float32)


def attend_kernel(pair, parts, tile, at_ref, seg_col, seg_row, q_ref, k_ref, v_ref, *refs):
    before_ref = refs[0] if pair else None
    o_ref, lse_ref = refs[-2:]
    head = pl.program_id(0)
    seq_me = at_ref[1]
    width = q_ref.shape[1]
    mine = head_lanes(width, head)
    half = jnp.bfloat16
    lanes = slice(pair * width, (pair + 1) * width)

    if pair:

        @pl.when(head == 0)
        def _():
            o_ref[:, : pair * width] = before_ref[...]

    def rows(i):
        return pl.ds(pl.multiple_of((seq_me ^ i) * tile, tile), tile)

    for i in range(parts):
        q = jnp.where(mine, q_ref[rows(i), :] * SCORE_SCALE, 0).astype(half)
        own = seg_col[i * tile : (i + 1) * tile, :]
        scores = []
        for j in range(i + 1):
            s = dot_rows(q, k_ref[rows(j), :])
            seen = own == seg_row[:, j * tile : (j + 1) * tile]
            if j == i:
                at = lax.broadcasted_iota(jnp.int32, (tile, tile), 0)
                seen = seen & (lax.broadcasted_iota(jnp.int32, (tile, tile), 1) <= at)
            scores.append(jnp.where(seen, s, -jnp.inf))
        top = scores[i].max(axis=-1, keepdims=True)
        for j in range(i):
            top = jnp.maximum(top, scores[j].max(axis=-1, keepdims=True))
        weights = [jnp.exp(s - top) for s in scores]
        total = weights[0].sum(axis=-1, keepdims=True)
        for w in weights[1:]:
            total = total + w.sum(axis=-1, keepdims=True)
        scale = 1.0 / total
        out = None
        for j in range(i + 1):
            term = jnp.dot(
                (weights[j] * scale).astype(half), v_ref[rows(j), :],
                preferred_element_type=jnp.float32,
            )
            out = term if out is None else out + term
        out = out.astype(half)
        o_ref[rows(i), lanes] = jnp.where(mine, out, o_ref[rows(i), lanes])
        log_total = jnp.broadcast_to(top + jnp.log(total), (tile, 128)).T
        lse_ref[0, :, i * tile : (i + 1) * tile] = log_total[:8]


def attend(pair, before, queries, keys, values, segments, at, seq_parts):
    full_len, width = queries.shape
    tile = full_len // seq_parts
    lanes = pair_width(width)
    heads = lanes // HEAD_DIM

    def whole(shape):
        return pl.BlockSpec(shape, lambda h, at: (0,) * len(shape))

    return pl.pallas_call(
        functools.partial(attend_kernel, pair, seq_parts, tile),
        grid_spec=pltpu.PrefetchScalarGridSpec(
            num_scalar_prefetch=1,
            grid=(heads,),
            in_specs=[whole((full_len, 1)), whole((1, full_len))]
            + [pl.BlockSpec((full_len, lanes), lambda h, at: (0, pair)) for _ in range(3)]
            + [whole(b.shape) for b in before],
            out_specs=[
                whole((full_len, (pair + 1) * lanes)),
                pl.BlockSpec((1, 8, full_len), lambda h, at: (h, 0, 0)),
            ],
        ),
        out_shape=[
            jax.ShapeDtypeStruct((full_len, (pair + 1) * lanes), jnp.bfloat16),
            jax.ShapeDtypeStruct((heads, 8, full_len), jnp.float32),
        ],
        cost_estimate=pl.CostEstimate(
            flops=8 * full_len * full_len * lanes,
            bytes_accessed=8 * full_len * lanes,
            transcendentals=full_len * full_len * heads // 2,
        ),
    )(at, segments[:, None], segments[None], queries, keys, values, *before)


def one_term_kernel(tile, *refs):
    left_ref, weight_ref, outs = refs[0], refs[1], refs[2:]
    for k, out_ref in enumerate(outs):
        rows = slice(k * tile, (k + 1) * tile)
        out_ref[...] = dot_rows(left_ref[rows, :], weight_ref[...]).astype(out_ref.dtype)


def one_term(part, count, left, weight, tile):
    columns, depth = weight.shape
    return pl.pallas_call(
        functools.partial(one_term_kernel, tile),
        grid=(1,),
        in_specs=[
            pl.BlockSpec((count * tile, depth), lambda i: (part, 0)),
            pl.BlockSpec((columns, depth), lambda i: (0, 0)),
        ],
        out_specs=[pl.BlockSpec((tile, columns), lambda i: (0, 0))] * count,
        out_shape=[jax.ShapeDtypeStruct((tile, columns), jnp.bfloat16)] * count,
        cost_estimate=pl.CostEstimate(
            flops=2 * count * tile * columns * depth,
            bytes_accessed=2 * columns * depth,
            transcendentals=0,
        ),
    )(left, weight)


def attend_back_kernel(
    pair, parts, tile, at_ref, seg_col, seg_row, q_ref, k_ref, v_ref, o_ref, do_ref, lse_ref, *refs
):
    before_ref = refs[0] if pair else None
    grad_ref, sum_ref, dq_ref, dk_ref, dv_ref = refs[-5:]
    head = pl.program_id(0)
    seq_me = at_ref[1]
    width = q_ref.shape[1]
    mine = head_lanes(width, head)
    half = jnp.bfloat16

    @pl.when(head == 0)
    def _():
        dq_ref[...] = jnp.zeros_like(dq_ref)
        dk_ref[...] = jnp.zeros_like(dk_ref)
        dv_ref[...] = jnp.zeros_like(dv_ref)
        if pair:
            grad_ref[:, : 3 * pair * width] = before_ref[...]

    def rows(i):
        return pl.ds(pl.multiple_of((seq_me ^ i) * tile, tile), tile)

    for i in range(parts):
        q = jnp.where(mine, q_ref[rows(i), :], 0)
        q_scaled = q * jnp.asarray(SCORE_SCALE, half)
        do = jnp.where(mine, do_ref[rows(i), :], 0)
        own = seg_row[:, i * tile : (i + 1) * tile]
        log_total = lse_ref[0, :1, i * tile : (i + 1) * tile]
        product = do.astype(jnp.float32) * o_ref[rows(i), :].astype(jnp.float32)
        row_dot = jnp.broadcast_to(jnp.sum(product, axis=-1, keepdims=True), (tile, 128)).T[:1]
        dq = None
        for j in range(i + 1):
            k = k_ref[rows(j), :]
            s = dot_rows(k, q_scaled)
            seen = seg_col[j * tile : (j + 1) * tile, :] == own
            if j == i:
                at = lax.broadcasted_iota(jnp.int32, (tile, tile), 0)
                seen = seen & (at <= lax.broadcasted_iota(jnp.int32, (tile, tile), 1))
            prob = jnp.where(seen, jnp.exp(s - log_total), 0.0)
            dv_ref[rows(j), :] += jnp.dot(prob.astype(half), do, preferred_element_type=jnp.float32)
            dp = dot_rows(v_ref[rows(j), :], do)
            ds = (prob * (dp - row_dot) * SCORE_SCALE).astype(half)
            dk_ref[rows(j), :] += jnp.dot(ds, q, preferred_element_type=jnp.float32)
            term = dot_first(ds, k)
            dq = term if dq is None else dq + term
        dq_ref[rows(i), :] += jnp.where(mine, dq, 0.0)

    @pl.when(head == pl.num_programs(0) - 1)
    def _():
        for c, ref in enumerate((dq_ref, dk_ref, dv_ref)):
            value = ref[...]
            to = (3 * pair + c) * width
            grad_ref[:, to : to + width] = value.astype(half)
            if c != 1:
                spot = 0 if c == 0 else 1
                sum_ref[spot : spot + 1, :] = jnp.sum(value, axis=0, keepdims=True)


def attend_back(
    pair, before, queries, keys, values, attended, grads, log_totals, segments, at, seq_parts
):
    full_len, width = queries.shape
    tile = full_len // seq_parts
    lanes = pair_width(width)
    heads = lanes // HEAD_DIM

    def whole(shape):
        return pl.BlockSpec(shape, lambda h, at: (0,) * len(shape))

    def of_pair():
        return pl.BlockSpec((full_len, lanes), lambda h, at: (0, pair))

    return pl.pallas_call(
        functools.partial(attend_back_kernel, pair, seq_parts, tile),
        grid_spec=pltpu.PrefetchScalarGridSpec(
            num_scalar_prefetch=1,
            grid=(heads,),
            in_specs=[whole((full_len, 1)), whole((1, full_len))]
            + [of_pair() for _ in range(5)]
            + [pl.BlockSpec((1, 8, full_len), lambda h, at: (h, 0, 0))]
            + [whole(b.shape) for b in before],
            out_specs=[whole((full_len, 3 * (pair + 1) * lanes)), whole((8, lanes))],
            scratch_shapes=[pltpu.VMEM((full_len, lanes), jnp.float32)] * 3,
        ),
        out_shape=[
            jax.ShapeDtypeStruct((full_len, 3 * (pair + 1) * lanes), jnp.bfloat16),
            jax.ShapeDtypeStruct((8, lanes), jnp.float32),
        ],
        cost_estimate=pl.CostEstimate(
            flops=20 * full_len * full_len * lanes,
            bytes_accessed=16 * full_len * lanes,
            transcendentals=full_len * full_len * heads // 2,
        ),
    )(
        at, segments[:, None], segments[None], queries, keys, values, attended, grads, log_totals,
        *before,
    )


def per_device(
    inputs,
    segments,
    ln1_gain,
    ln1_bias,
    qkv_weight,
    query_bias,
    value_bias,
    out_weight,
    out_bias,
    ln2_gain,
    ln2_bias,
    up_weight,
    up_bias,
    down_weight,
    down_bias,
    cotangent,
):
    half = jnp.bfloat16
    wide = jnp.float32
    seq_count, group_len, model_width = inputs.shape
    assert seq_count == 1
    dp_parts, seq_parts = lax.axis_size(DP), lax.axis_size(SEQ)
    dp_me, seq_me = lax.axis_index(DP), lax.axis_index(SEQ)
    at = jnp.stack([dp_me, seq_me]).astype(jnp.int32)
    order = mask_order(dp_parts)
    head_width = model_width // seq_parts
    block = qkv_weight.shape[0]
    down_block = down_weight.shape[0]
    unit_width = dp_parts * down_block
    span = dp_parts // seq_parts

    out_moves = []
    for d in range(dp_parts):
        for s in range(seq_parts):
            source = d * seq_parts + s
            out_moves.append((source, ((d % span) * seq_parts + s) * seq_parts + d // span))

    tokens = inputs.reshape(group_len, model_width)
    pieces = qkv_pieces(qkv_weight, seq_parts, at)
    qkv_mine = jnp.stack([pieces[0]] + [swap(pieces[k], SEQ, k) for k in range(1, seq_parts)])
    tokens_far = rows_far(tokens, seq_parts)
    out_moved = lax.ppermute(out_weight, (DP, SEQ), out_moves)
    out_chunk = vector_row(
        out_moved,
        [
            ln1_gain,
            ln1_bias,
            query_bias,
            value_bias,
            out_bias,
            ln2_gain,
            ln2_bias,
            down_bias,
            up_bias,
        ],
    )
    out_outer = gather_outer(out_chunk, dp_parts)
    qkv_outer = gather_outer(qkv_mine, dp_parts)
    pieces = up_pieces(up_weight, dp_parts, seq_parts, at)
    up_mine = jnp.stack([pieces[0]] + [swap(pieces[k], SEQ, k) for k in range(1, seq_parts)])
    qkv_groups = gather_inner(qkv_outer, dp_parts)
    qkv_cols = qkv_place(qkv_groups, dp_parts, at).reshape(model_width, 3 * head_width)
    tokens_parts = rows_near(tokens, tokens_far, seq_parts)[2]

    out_part, vectors = out_place(gather_inner(out_outer, dp_parts), block, dp_parts, at)
    out_part = out_part.reshape(head_width, model_width)
    vectors = vectors[:, 0, : 8 * block + down_block]
    bias_up = place_dp(vectors[:, 8 * block :], dp_me, order).reshape(unit_width)
    vectors = vectors[:, : 8 * block].astype(half)
    table = place_by(
        [vectors] + [swap(vectors, SEQ, k) for k in range(1, seq_parts)], seq_me
    ).astype(wide)
    table = table.reshape(seq_parts, dp_parts, 8, block).transpose(2, 1, 0, 3)
    table = table.reshape(8, model_width)
    (gain_one, bias_one, bias_query, bias_value, bias_out, gain_two, bias_two, bias_down) = (
        table[i] for i in range(8)
    )

    up_outer = gather_outer(up_mine, dp_parts)
    query_part = lax.dynamic_slice_in_dim(bias_query, seq_me * head_width, head_width, 0)
    value_part = lax.dynamic_slice_in_dim(bias_value, seq_me * head_width, head_width, 0)
    upstream = cotangent.reshape(group_len, model_width)
    upstream_near, upstream_rest, upstream_parts = rows_near(
        upstream, rows_far(upstream, seq_parts), seq_parts
    )

    normed_full, queries, keys_mine, values_mine = project(
        tokens_parts, gain_one, bias_one, qkv_cols, query_part, value_part
    )
    up_groups = gather_inner(up_outer, dp_parts)
    up_cols = up_place(up_groups, dp_parts, down_block, at).reshape(model_width, unit_width)
    down_outer = gather_outer(down_weight, dp_parts)
    down_part = join(gather_inner(down_outer, dp_parts)).reshape(unit_width, model_width)
    pairs = head_width // pair_width(head_width)
    before, log_totals = [], []
    for p in range(pairs):
        attended, log_total = attend(
            p, before, queries, keys_mine, values_mine, segments[0], at, seq_parts
        )
        before = [attended]
        log_totals.append(log_total)

    def block_dots(rows, weight):
        found = [None] * seq_parts
        for k in reversed(range(seq_parts)):
            found[k] = jnp.dot(
                rows[k * group_len : (k + 1) * group_len], weight, preferred_element_type=wide
            ).astype(half)
        return found

    hidden_in = tokens.astype(wide)
    attended_sum = rows_out(block_dots(attended, out_part), seq_parts)[0]
    residual_one = hidden_in + attended_sum + bias_out
    normed_two, unit_two, inverse_two = layer_norm(residual_one, gain_two, bias_two)
    normed_two = normed_two.astype(half)
    normed_two_near, normed_two_rest, normed_two_parts = rows_near(
        normed_two, rows_far(normed_two, seq_parts), seq_parts
    )

    def feed(normed_rows, upstream_rows):
        preact = jnp.dot(normed_rows, up_cols, preferred_element_type=wide) + bias_up
        activated, derivative = gelu_pair(preact)
        preact_grad = jnp.dot(upstream_rows, down_part.T, preferred_element_type=wide) * derivative
        preact_half = preact_grad.astype(half)
        two = [
            jnp.dot(
                preact_half[i : i + group_len], up_cols.T, preferred_element_type=wide
            ).astype(half)
            for i in range(0, preact_half.shape[0], group_len)
        ]
        return activated.astype(half), preact_half, two, jnp.sum(preact_grad, axis=0)

    act_near, preact_near, two_near, up_b_near = feed(normed_two_near, upstream_near)
    act_rest, preact_rest, two_rest, up_b_rest = feed(normed_two_rest, upstream_rest)
    grad_up_b = up_b_near + up_b_rest
    normed_two_grad, two_sent = rows_out(two_near + two_rest, seq_parts)

    act_near, act_rest, preact_near, preact_rest = lax.optimization_barrier(
        (act_near, act_rest, preact_near, preact_rest, *two_sent)
    )[:4]
    inner = inner_of(dp_parts)
    grad_down = token_grad((act_near, act_rest), upstream_parts, False, dp_parts, down_block, at)
    down_terms = scatter_outer(scatter_inner(grad_down, dp_parts), dp_parts, half)
    grad_up = token_grad(
        normed_two_parts,
        (after(preact_near, grad_down[-1]), preact_rest),
        True,
        dp_parts,
        down_block,
        at,
    )

    upstream_wide = cotangent.astype(wide).reshape(group_len, model_width)
    residual_grad = upstream_wide + layer_norm_back(
        normed_two_grad, unit_two, inverse_two, gain_two
    )
    residual_half = residual_grad.astype(half)
    residual_far = rows_far(residual_half, seq_parts)
    residual_near, residual_rest, _ = rows_near(residual_half, residual_far, seq_parts)
    residual_full = jnp.concatenate([residual_near, residual_rest])
    attended_grad = jnp.concatenate(
        [
            jnp.dot(r, out_part.T, preferred_element_type=wide).astype(half)
            for r in (residual_near, residual_rest)
        ]
    )
    grad_out = jnp.dot(attended.T, residual_full, preferred_element_type=wide).astype(half)
    grad_out = grad_out.reshape(dp_parts, block, model_width)
    before, head_sums, qkv_terms, earlier = [], [], [], []
    for p in range(pairs):
        qkv_half, sums = attend_back(
            p,
            before,
            after(queries, *earlier),
            keys_mine,
            values_mine,
            attended,
            attended_grad,
            log_totals[p],
            segments[0],
            at,
            seq_parts,
        )
        before = [qkv_half]
        head_sums.append(sums)
        packed = qkv_grad(normed_full, qkv_half, grad_out, p, seq_parts, at)
        qkv_terms.append((packed, scatter_inner(packed, dp_parts)))
        earlier = packed
        if p == 0:
            up_part = scatter_inner(grad_up, dp_parts, qkv_half)
            up_terms = scatter_outer(up_part, dp_parts, half)
    one_blocks = []
    for part in (0, 1):
        count = seq_parts - 2 if part else 2
        if seq_parts == 4:
            one_blocks += one_term(part, count, qkv_half, qkv_cols, group_len)
        else:
            one_blocks += [
                jnp.dot(
                    qkv_half[k * group_len : (k + 1) * group_len],
                    qkv_cols.T,
                    preferred_element_type=wide,
                ).astype(half)
                for k in (range(2, seq_parts) if part else range(2))
            ]
    normed_one_grad, _ = rows_out(one_blocks, seq_parts)
    down_out = [
        jnp.dot(
            after(a, up_part)[i : i + group_len], down_part, preferred_element_type=wide
        ).astype(half)
        for a in (act_near, act_rest)
        for i in range(0, a.shape[0], group_len)
    ]
    down_sum = rows_out(down_out, seq_parts)[0]
    outputs = (residual_one + down_sum + bias_down).astype(half)
    _, unit_one, inverse_one = layer_norm(hidden_in, gain_one, bias_one)
    input_grad = residual_grad + layer_norm_back(normed_one_grad, unit_one, inverse_one, gain_one)

    query_sums = jnp.concatenate([sums[0] for sums in head_sums])
    value_sums = jnp.concatenate([sums[1] for sums in head_sums])

    def place_part(part):
        return lax.dynamic_update_slice_in_dim(
            jnp.zeros((model_width,), wide), part, seq_me * head_width, 0
        )

    early = jnp.stack(
        [
            place_part(query_sums),
            place_part(value_sums),
            jnp.sum(residual_grad, axis=0),
            jnp.sum(normed_two_grad * unit_two, axis=0),
            jnp.sum(normed_two_grad, axis=0),
            jnp.sum(upstream_wide, axis=0),
        ]
    )
    late = jnp.stack(
        [jnp.sum(normed_one_grad * unit_one, axis=0), jnp.sum(normed_one_grad, axis=0)]
    )
    found = [None] * dp_parts
    for m, mask in enumerate(order):
        found[mask] = grad_up_b.reshape(dp_parts, down_block)[m]
    grad_up_b = place_by(found, dp_me).reshape(1, unit_width)
    grad_up_b = jnp.pad(grad_up_b, ((0, 0), (0, model_width - unit_width)))

    def add_over(small, axis, parts):
        mask = 1
        while mask < parts:
            small = small + swap(small, axis, mask)
            mask *= 2
        return small

    small = add_over(jnp.concatenate([late, early]), SEQ, seq_parts)
    small = add_over(jnp.concatenate([small, grad_up_b]), DP, dp_parts)

    terms = [scatter_outer(part, dp_parts, half) for _, part in qkv_terms]
    *columns, out_rows = qkv_sum(terms, seq_parts, at)
    found = [columns[0]] + [swap(columns[k], SEQ, k) for k in range(1, seq_parts)]
    out_share = lax.ppermute(
        out_rows, (DP, SEQ), [(b, a) for a, b in out_moves]
    ).astype(wide)
    qkv_share = qkv_finish(found, at)
    down_share = total_of(down_terms)
    up_rows = total_of(up_terms).astype(half)
    up_rows = up_rows.reshape(seq_parts, block, unit_width)
    up_share = up_finish(
        exchange_seq(
            lambda t: lax.dynamic_index_in_dim(up_rows, t, 0, keepdims=False), seq_me, seq_parts
        ),
        dp_parts,
        seq_parts,
        at,
    )
    spot = (dp_me * seq_parts + seq_me) * block
    own = lax.dynamic_slice_in_dim(small[:8], spot, block, 1)
    shares = [own[i] for i in range(8)]
    share_up_b = lax.dynamic_slice_in_dim(small[8], dp_me * down_block, down_block, 0)

    return (
        outputs[None],
        input_grad[None],
        shares[0],
        shares[1],
        qkv_share,
        shares[2],
        shares[3],
        out_share,
        shares[4],
        shares[5],
        shares[6],
        up_share,
        share_up_b,
        down_share,
        shares[7],
    )


def solution(mesh):
    spread = (DP, SEQ)
    vector, matrix, rows = P(spread), P(spread, None), P(DP, SEQ, None)
    return jax.shard_map(
        per_device,
        mesh=mesh,
        in_specs=(
            rows,
            P(DP, None),
            vector,
            vector,
            matrix,
            vector,
            vector,
            matrix,
            vector,
            vector,
            vector,
            matrix,
            vector,
            matrix,
            vector,
            rows,
        ),
        out_specs=(
            rows,
            rows,
            vector,
            vector,
            matrix,
            vector,
            vector,
            matrix,
            vector,
            vector,
            vector,
            matrix,
            vector,
            matrix,
            vector,
        ),
        check_vma=False,
    )
```
